512 devices in a mesh: ex: 16 (over z), feat: 32 (over y, x, core).
Axes of the slice: x: 4, y: 4, z: 16, core: 2. Of those that a mesh axis runs over, the one named last changes fastest.
Arguments:
- dosages: bfloat16 [65536, 4096], P('ex', 'feat'), may hold values from -6 to 6
- coefficients: bfloat16 [4096], P('feat'), may hold values from -0.046875 to 0.046875
- directions: bfloat16 [4096, 128], P('feat'), may hold values from -6 to 6
- event_rank: int32 [65536], P('ex'), may hold values from 0 to 65535, as said below
- events: int32 [65536], P('ex'), may hold values from 0 to 1, as said below
Outputs:
- hessian_product: float32 [4096, 128], P('feat')
The draws below stay inside these ranges and needn't reach their ends.
Inputs may be any that keep to these rules, and one draw needn't show every extreme that they name: `event_rank`: the 4096 persons of each aligned block b (one index of ex) hold the ranks b * 4096 to (b + 1) * 4096 - 1, each once, in any order. `events`: the first person of every aligned block of 4096 persons has an event.
All inputs are finite; a program needn't handle non-finite values.
Results may differ from the reference program's by a relative error of at most 0.00084.
Values may be sent and summed in bfloat16 or wider, within the bound.
A program may use at most 64 MiB of HBM per device.

```python
import jax
import jax.numpy as jnp

P_SIZE = 4096
K = 128
ROWS = 4096
PERSONS = 65536


def draw_dosages(key, part):
    blocks = PERSONS // ROWS
    spread = jax.random.normal(jax.random.fold_in(key, 3), (P_SIZE,), jnp.float32)
    block_of = (jnp.arange(PERSONS, dtype=jnp.int32) // ROWS).astype(jnp.float32)
    level = 2.0 * block_of / max(blocks - 1, 1) - 1.0
    noise = jax.random.normal(jax.random.fold_in(key, 5), (PERSONS, P_SIZE), jnp.float32)
    amplitude = 0.5
    values = noise + amplitude * level[:, None] * spread[None, :]
    return jnp.clip(values, -6.0, 6.0).astype(jnp.bfloat16)


def draw_event_rank(key, part):
    blocks = PERSONS // ROWS
    orders = jax.vmap(lambda number: jax.random.permutation(jax.random.fold_in(key, number), ROWS))(jnp.arange(blocks))
    return (orders + jnp.arange(blocks)[:, None] * ROWS).reshape(-1).astype(jnp.int32)


def draw_events(key, part):
    position = jnp.arange(PERSONS, dtype=jnp.int32)
    limit = 100 + 400 * position // PERSONS
    drawn = jax.random.randint(jax.random.fold_in(key, 7), (PERSONS,), 0, 1000)
    return ((drawn < limit) | (position % ROWS == 0)).astype(jnp.int32)


def block_levels(rng, shape, shards, low, high):
    level, own = 1.0, jax.random.fold_in(rng, 6)
    for dim, parts in shards:
        steps = jnp.exp(jax.random.uniform(jax.random.fold_in(own, dim), (parts,), jnp.float32, low / len(shards), high / len(shards)))
        level = level * jnp.repeat(steps, shape[dim] // parts).reshape([-1 if axis == dim else 1 for axis in range(len(shape))])
    return level


def centred(rng, shape, width, most, cuts=(), kind=jnp.bfloat16):
    array = jax.random.normal(rng, shape, jnp.float32) * width
    if len(cuts) > 0:
        array = block_levels(rng, shape, cuts, -0.22, 0.18) * array
    return jnp.clip(array, min=-most, max=most).astype(kind)


def setup_inputs(seed: int = 0) -> dict:
    keys = jax.random.split(jax.random.key(seed), 6)
    return {
        "dosages": draw_dosages(jax.random.fold_in(keys[5], 71), 0),
        "coefficients": centred(keys[1], (P_SIZE,), (4 * P_SIZE) ** -0.5, 0.046875, ((0, 32),)),
        "directions": centred(keys[2], (P_SIZE, K), 1.0, 6.0, ((0, 32),)),
        "event_rank": draw_event_rank(jax.random.fold_in(keys[5], 71), 0),
        "events": draw_events(jax.random.fold_in(keys[5], 71), 0),
    }


def reference(dosages, coefficients, directions, event_rank, events):
    linear = jnp.dot(dosages, coefficients, preferred_element_type=jnp.float32)
    risk = jnp.exp(linear)
    tangent = jnp.dot(dosages, directions, preferred_element_type=jnp.float32)
    weighted_t = tangent * risk[:, None]
    order = jnp.argsort(event_rank)
    risk_sorted = risk[order]
    tangent_sorted = weighted_t[order]
    event_sorted = events[order].astype(jnp.float32)
    risk_sum = jnp.cumsum(risk_sorted[::-1])[::-1]
    tangent_sum = jnp.cumsum(tangent_sorted[::-1], axis=0)[::-1]
    hazard = event_sorted / risk_sum
    hazard_tangent = tangent_sum * (event_sorted / (risk_sum * risk_sum))[:, None]
    cumulative = jnp.cumsum(hazard)[event_rank]
    cumulative_tangent = jnp.cumsum(hazard_tangent, axis=0)[event_rank]
    weighted = (risk[:, None] * (tangent * cumulative[:, None] - cumulative_tangent)).astype(jnp.bfloat16)
    total = jnp.dot(dosages.T, weighted, preferred_element_type=jnp.float32)
    return total / jnp.sum(events.astype(jnp.float32))
```

```python
import functools

import jax
import jax.numpy as jnp
from jax import lax
from jax.experimental import pallas as pl
from jax.experimental.pallas import tpu as pltpu
from jax.sharding import PartitionSpec as P

MESH = pl.DeviceIdType.MESH
F32 = jnp.float32
BF16 = jnp.bfloat16
LO = 256


def row_of(tile):
    return jnp.concatenate([tile[i : i + 1, :] for i in range(tile.shape[0])], axis=1)


def split_pair(value):
    high = value.astype(BF16)
    return high, value - high.astype(F32)


def kernel(
    nz, n, d_hbm, coef_ref, dirs_ref, rank_ref, ev_ref, out_ref,
    d2, dirs2, coef2, tsend, lin1, recv1, rlin1, r2, lin2, recv2, rlin2,
    m1, hrep, hi8, lhs, t8s, risks, sel,
    z1, zr1, z2, zr2, abuf, pbuf, prec, ps, zr3, obuf,
    lsem, dsend, drecv, s1, q1, s1l, q1l, s2, q2, s2l, q2l,
    sz1, qz1, sz2, qz2, sa, qa, sb, qb, sp, qp, sz3, qz3, sz4, qz4,
):
    rows = d_hbm.shape[0]
    half, sub, hi_n = rows // 2, rows // 4, rows // LO
    z, f = lax.axis_index("ex"), lax.axis_index("feat")
    c, chip = lax.rem(f, 2), lax.div(f, 2)
    x, y = lax.rem(chip, n), lax.div(chip, n)
    other = 1 - c

    def at(yy, xx, cc):
        return {"feat": (yy * n + xx) * 2 + cc}

    partner = at(y, x, other)
    xs = [lax.rem(x + d, n) for d in range(n)]
    ys = [lax.rem(y + d, n) for d in range(n)]
    zs = [lax.rem(z + d, nz) for d in range(nz)]
    far = sorted(range(1, nz), key=lambda d: -min(d, nz - d))

    def remote(src, dst, send, recv, device):
        return pltpu.make_async_remote_copy(
            src_ref=src, dst_ref=dst, send_sem=send, recv_sem=recv,
            device_id=device, device_id_type=MESH,
        )

    barrier = pltpu.get_barrier_semaphore()
    for d in far:
        pl.semaphore_signal(barrier, inc=1, device_id={"ex": zs[d]}, device_id_type=MESH)
    for d in range(1, n):
        for cc in range(2):
            pl.semaphore_signal(barrier, inc=1, device_id=at(ys[d], x, cc), device_id_type=MESH)
            pl.semaphore_signal(barrier, inc=1, device_id=at(y, xs[d], cc), device_id_type=MESH)
    pl.semaphore_signal(barrier, inc=1, device_id=partner, device_id_type=MESH)

    lanes = pl.ds(pl.multiple_of(c * 128, 128), 128)
    own_d = pltpu.make_async_copy(
        d_hbm.at[pl.ds(pl.multiple_of(c * half, half), half)], d2.at[:, lanes], lsem.at[0]
    )
    own_d.start()
    own_dirs = pltpu.make_async_copy(dirs_ref, dirs2.at[c], lsem.at[1])
    own_dirs.start()
    own_coef = pltpu.make_async_copy(coef_ref, coef2.at[c], lsem.at[2])
    own_coef.start()

    place = row_of(rank_ref[...]) & (rows - 1)
    hi_b = jnp.broadcast_to(place >> 8, (8, rows))
    lo_b = jnp.broadcast_to(place & (LO - 1), (8, rows))
    hi8[...] = hi_b
    level = lax.broadcasted_iota(jnp.int32, (8, rows), 0)
    for block in range(LO // 16):
        upper = (lo_b >= level + block * 16).astype(F32)
        lower = (lo_b >= level + (block * 16 + 8)).astype(F32)
        m1[block * 16 : block * 16 + 16, :] = jnp.concatenate([upper, lower], 0).astype(BF16)
    for hi in range(hi_n):
        same = (hi_b == hi).astype(F32)
        hrep[hi] = jnp.concatenate([same, same], 0).astype(BF16)

    pl.semaphore_wait(barrier, (nz - 1) + 4 * (n - 1) + 1)

    away_d = remote(
        d_hbm.at[pl.ds(pl.multiple_of(other * half, half), half)], d2.at[:, lanes],
        dsend.at[0], drecv.at[0], partner,
    )
    away_dirs = remote(dirs_ref, dirs2.at[c], dsend.at[1], drecv.at[1], partner)
    away_coef = remote(coef_ref, coef2.at[c], dsend.at[2], drecv.at[2], partner)
    away_dirs.start()
    away_coef.start()
    away_d.start()

    ev = row_of(ev_ref[...]).astype(F32)
    ev16 = jnp.broadcast_to(ev, (16, rows)).astype(BF16)
    for hi in range(hi_n):
        lhs[hi * 16 : hi * 16 + 16, :] = ev16 * hrep[hi]
    over_both = (((1,), (1,)), ((), ()))
    late = lax.dot_general(
        lhs[: hi_n * 16, :], m1[...], over_both, preferred_element_type=F32
    ).reshape(hi_n, 16, LO)[:, :8, :].reshape(hi_n * 8, LO)
    lane = lax.broadcasted_iota(jnp.int32, (hi_n * 8, LO), 1)
    after = jnp.where(lane == LO - 1, 0.0, pltpu.roll(late, LO - 1, 1))
    happened = (late - after).reshape(hi_n, 8, LO)
    count_own = jnp.sum(ev, axis=1, keepdims=True)

    own_dirs.wait()
    own_coef.wait()
    own_d.wait()
    away_dirs.wait()
    away_coef.wait()
    away_d.wait()

    weights = jnp.concatenate(
        [dirs2[cc].astype(F32).T.astype(BF16) for cc in range(2)], axis=1
    )
    slopes = jnp.concatenate(
        [jnp.broadcast_to(coef2[cc].astype(F32), (16, 128)).astype(BF16) for cc in range(2)], axis=1
    )
    first = []
    for part in range(2):
        people = d2[part * sub : part * sub + sub, :]
        tsend[part] = lax.dot_general(
            weights, people, over_both, preferred_element_type=F32
        ).reshape(n, n, 8, sub)
        lin1[part] = lax.dot_general(slopes, people, over_both, preferred_element_type=F32)[0:1]
        for d in range(n - 1, 0, -1):
            if part == 0:
                source, device = tsend.at[0, xs[d]], at(y, xs[d], c)
            else:
                source, device = tsend.at[1, :, ys[d]], at(ys[d], x, c)
            a = remote(source, recv1.at[part, d], s1.at[part, d], q1.at[part, d], device)
            b = remote(lin1.at[part], rlin1.at[part, d], s1l.at[part, d], q1l.at[part, d], device)
            b.start()
            a.start()
            first += [a, b]
    for copy in first:
        copy.wait()

    second = []
    for part in range(2):
        if part == 0:
            total = tsend[0, x]
        else:
            total = tsend[1, :, y]
        line = lin1[part]
        for d in range(1, n):
            total = total + recv1[part, d]
            line = line + rlin1[part, d]
        r2[part] = total
        lin2[part] = line
        here = y if part == 0 else x
        recv2[part, c, 0] = r2[part, here]
        rlin2[part, c, 0] = line
        for d in range(n - 1, -1, -1):
            for cc in (c, other):
                if d == 0 and cc is c:
                    continue
                if part == 0:
                    source, device = r2.at[0, ys[d]], at(ys[d], x, cc)
                else:
                    source, device = r2.at[1, xs[d]], at(y, xs[d], cc)
                a = remote(source, recv2.at[part, c, d], s2.at[part, cc, d], q2.at[part, c, d], device)
                b = remote(lin2.at[part], rlin2.at[part, c, d], s2l.at[part, cc, d], q2l.at[part, c, d], device)
                b.start()
                a.start()
                second += [a, b]
    for copy in second:
        copy.wait_send()
    for part in range(2):
        for d in range(n):
            for cc in (c, other):
                if d == 0 and cc is c:
                    continue
                device = partner
                remote(r2.at[part, 0], recv2.at[part, cc, d], s2.at[part, cc, d], q2.at[part, cc, d], device).wait_recv()
                remote(lin2.at[part], rlin2.at[part, cc, d], s2l.at[part, cc, d], q2l.at[part, cc, d], device).wait_recv()

    for cc in range(2):
        for part in range(2):
            span = slice((cc * 2 + part) * sub, (cc * 2 + part + 1) * sub)
            total, line = recv2[part, cc, 0], rlin2[part, cc, 0]
            for d in range(1, n):
                total = total + recv2[part, cc, d]
                line = line + rlin2[part, cc, d]
            risk = jnp.exp(jnp.broadcast_to(line, (8, sub)))
            t8s[:, span] = total
            risks[:, span] = risk
            wt = total * risk
            _, wt_low = split_pair(wt)
            _, risk_low = split_pair(risk)
            pieces = jnp.concatenate([wt, wt_low, risk, risk_low], 0).astype(BF16)
            for hi in range(hi_n):
                mask = hrep[hi, :, span]
                lhs[hi * 32 : hi * 32 + 16, span] = pieces[:16] * mask
                lhs[hi * 32 + 16 : hi * 32 + 32, span] = pieces[16:] * mask

    inside = lax.dot_general(
        lhs[...], m1[...], over_both, preferred_element_type=F32
    ).reshape(hi_n, 32, LO)
    inside_t = inside[:, 0:8] + inside[:, 8:16]
    inside_r = inside[:, 16:24] + inside[:, 24:32]
    carry_t, carry_r = [None] * hi_n, [None] * hi_n
    sum_t = jnp.zeros((8, 1), F32)
    sum_r = jnp.zeros((8, 1), F32)
    for hi in range(hi_n - 1, -1, -1):
        carry_t[hi], carry_r[hi] = sum_t, sum_r
        sum_t = sum_t + inside_t[hi][:, 0:1]
        sum_r = sum_r + inside_r[hi][:, 0:1]

    lane8 = lax.broadcasted_iota(jnp.int32, (8, 128), 1)
    diag = lane8 == lax.broadcasted_iota(jnp.int32, (8, 128), 0)
    lane1 = lax.broadcasted_iota(jnp.int32, (1, 128), 1)

    def to_row(col_t, col_r):
        row = jnp.sum(jnp.where(diag, jnp.broadcast_to(col_t, (8, 128)), 0.0), axis=0, keepdims=True)
        return row + jnp.where(lane1 == 8, jnp.broadcast_to(col_r[0:1], (1, 128)), 0.0)

    def to_cols(row):
        wide = jnp.broadcast_to(row, (8, 128))
        col_t = jnp.sum(jnp.where(diag, wide, 0.0), axis=1, keepdims=True)
        col_r = jnp.sum(jnp.where(lane8 == 8, wide, 0.0), axis=1, keepdims=True)
        return col_t, col_r

    z1[...] = to_row(sum_t, sum_r) + jnp.where(lane1 == 9, jnp.broadcast_to(count_own, (1, 128)), 0.0)
    carry = []
    for d in far:
        copy = remote(z1, zr1.at[d], sz1.at[d], qz1.at[d], {"ex": zs[d]})
        copy.start()
        carry.append(copy)
    for copy in carry:
        copy.wait()
    later = jnp.zeros((1, 128), F32)
    every = z1[...]
    for d in range(1, nz):
        sender = lax.rem(z + nz - d, nz)
        got = zr1[d]
        every = every + got
        later = later + jnp.where(sender > z, got, 0.0)
    later_t, later_r = to_cols(later)
    count = jnp.sum(jnp.where(lane1 == 9, every, 0.0), axis=1, keepdims=True)

    run_t = jnp.zeros((8, 1), F32)
    run_r = jnp.zeros((8, 1), F32)
    before, rates = [], []
    for hi in range(hi_n):
        at_risk = inside_r[hi] + (carry_r[hi] + later_r)
        moment = inside_t[hi] + (carry_t[hi] + later_t)
        hazard = happened[hi] / at_risk
        hazard_t = moment * (happened[hi] / (at_risk * at_risk))
        before.append(jnp.concatenate([run_t, run_r], 0))
        rates += [hazard_t, hazard]
        run_t = run_t + jnp.sum(hazard_t, axis=1, keepdims=True)
        run_r = run_r + jnp.sum(hazard, axis=1, keepdims=True)
    z2[...] = to_row(run_t, run_r)
    carry = []
    for d in far:
        copy = remote(z2, zr2.at[d], sz2.at[d], qz2.at[d], {"ex": zs[d]})
        copy.start()
        carry.append(copy)

    rate, rate_low = split_pair(jnp.concatenate(rates, 0))
    rate_low = rate_low.astype(BF16)
    width = min(512, half)
    for chunk in range(half // width):
        begin = pl.multiple_of(c * half + chunk * width, width)
        member = m1[:, pl.ds(begin, width)]
        spread = jnp.dot(rate, member, preferred_element_type=F32) + jnp.dot(
            rate_low, member, preferred_element_type=F32
        )
        spot = hi8[:, pl.ds(begin, width)]
        spot = jnp.concatenate([spot, spot], 0)
        chosen = jnp.zeros((16, width), F32)
        for hi in range(hi_n):
            chosen = jnp.where(spot == hi, spread[hi * 16 : hi * 16 + 16] + before[hi], chosen)
        sel[:, chunk * width : (chunk + 1) * width] = chosen

    for copy in carry:
        copy.wait()
    early = jnp.zeros((1, 128), F32)
    for d in range(1, nz):
        sender = lax.rem(z + nz - d, nz)
        early = early + jnp.where(sender < z, zr2[d], 0.0)
    early_t, early_r = to_cols(early)

    gather = []
    for part in range(2):
        span = slice(part * sub, part * sub + sub)
        begin = pl.multiple_of(c * half + part * sub, sub)
        tangent, risk = t8s[:, pl.ds(begin, sub)], risks[:, pl.ds(begin, sub)]
        weighted = risk * (tangent * (sel[8:16, span] + early_r) - (sel[0:8, span] + early_t))
        abuf[part, x, y] = weighted.astype(BF16)
        for d in range(n - 1, 0, -1):
            device = at(ys[d], x, c) if part == 0 else at(y, xs[d], c)
            copy = remote(abuf.at[part, x, y], abuf.at[part, x, y], sa.at[part, d], qa.at[part, d], device)
            copy.start()
            gather.append(copy)
    for copy in gather:
        copy.wait_send()
    for part in range(2):
        for d in range(1, n):
            back = lax.rem((y if part == 0 else x) + n - d, n)
            slot = abuf.at[0, x, back] if part == 0 else abuf.at[1, back, y]
            remote(slot, slot, sa.at[part, d], qa.at[part, d], partner).wait_recv()
    gather = []
    for part in range(2):
        source = abuf.at[0, x] if part == 0 else abuf.at[1, :, y]
        for d in range(n - 1, 0, -1):
            device = at(y, xs[d], c) if part == 0 else at(ys[d], x, c)
            copy = remote(source, source, sb.at[part, d], qb.at[part, d], device)
            copy.start()
            gather.append(copy)
    for copy in gather:
        copy.wait_send()
    for part in range(2):
        for d in range(1, n):
            back = lax.rem((x if part == 0 else y) + n - d, n)
            slot = abuf.at[0, back] if part == 0 else abuf.at[1, :, back]
            remote(slot, slot, sb.at[part, d], qb.at[part, d], partner).wait_recv()

    k_n = n * n * 8
    product = jnp.zeros((k_n, 256), F32)
    for part in range(2):
        product = product + jnp.dot(
            abuf[part].reshape(k_n, sub), d2[part * sub : part * sub + sub, :],
            preferred_element_type=F32,
        )
    pbuf[0] = product[:, :128]
    pbuf[1] = product[:, 128:]
    swap = remote(pbuf.at[other], prec, sp, qp, partner)
    swap.start()
    swap.wait()
    share = k_n // nz
    ps[...] = (pbuf[c] + prec[...]).reshape(nz, share, 128)
    carry = []
    for d in far:
        copy = remote(ps.at[zs[d]], zr3.at[d], sz3.at[d], qz3.at[d], {"ex": zs[d]})
        copy.start()
        carry.append(copy)
    for copy in carry:
        copy.wait()
    done = ps[z]
    for d in range(1, nz):
        done = done + zr3[d]
    obuf[z] = done / count
    carry = []
    for d in far:
        copy = remote(obuf.at[z], obuf.at[z], sz4.at[d], qz4.at[d], {"ex": zs[d]})
        copy.start()
        carry.append(copy)
    for copy in carry:
        copy.wait_send()
    for d in far:
        back = lax.rem(z + nz - d, nz)
        remote(obuf.at[back], obuf.at[back], sz4.at[d], qz4.at[d], {"ex": zs[d]}).wait_recv()
    out_ref[...] = obuf[...].reshape(k_n, 128).T


def local(nz, n, dosages, coefficients, directions, event_rank, events):
    rows, feats = dosages.shape
    k_n = directions.shape[1]
    sub, half, hi_n = rows // 4, rows // 2, rows // LO
    vmem = pl.BlockSpec(memory_space=pltpu.VMEM)
    dma = pltpu.SemaphoreType.DMA
    return pl.pallas_call(
        functools.partial(kernel, nz, n),
        out_shape=jax.ShapeDtypeStruct((feats, k_n), F32),
        in_specs=[pl.BlockSpec(memory_space=pl.ANY)] + [vmem] * 4,
        out_specs=vmem,
        scratch_shapes=[
            pltpu.VMEM((half, 2 * feats), BF16),
            pltpu.VMEM((2, feats, k_n), BF16),
            pltpu.VMEM((2, 1, feats), BF16),
            pltpu.VMEM((2, n, n, 8, sub), F32),
            pltpu.VMEM((2, 1, sub), F32),
            pltpu.VMEM((2, n, n, 8, sub), F32),
            pltpu.VMEM((2, n, 1, sub), F32),
            pltpu.VMEM((2, n, 8, sub), F32),
            pltpu.VMEM((2, 1, sub), F32),
            pltpu.VMEM((2, 2, n, 8, sub), F32),
            pltpu.VMEM((2, 2, n, 1, sub), F32),
            pltpu.VMEM((LO, rows), BF16),
            pltpu.VMEM((hi_n, 16, rows), BF16),
            pltpu.VMEM((8, rows), jnp.int32),
            pltpu.VMEM((hi_n * 32, rows), BF16),
            pltpu.VMEM((8, rows), F32),
            pltpu.VMEM((8, rows), F32),
            pltpu.VMEM((16, half), F32),
            pltpu.VMEM((1, 128), F32),
            pltpu.VMEM((nz, 1, 128), F32),
            pltpu.VMEM((1, 128), F32),
            pltpu.VMEM((nz, 1, 128), F32),
            pltpu.VMEM((2, n, n, 8, sub), BF16),
            pltpu.VMEM((2, k_n, 128), F32),
            pltpu.VMEM((k_n, 128), F32),
            pltpu.VMEM((nz, k_n // nz, 128), F32),
            pltpu.VMEM((nz, k_n // nz, 128), F32),
            pltpu.VMEM((nz, k_n // nz, 128), F32),
            dma((3,)), dma((3,)), dma((3,)),
            dma((2, n)), dma((2, n)), dma((2, n)), dma((2, n)),
            dma((2, 2, n)), dma((2, 2, n)), dma((2, 2, n)), dma((2, 2, n)),
            dma((nz,)), dma((nz,)), dma((nz,)), dma((nz,)),
            dma((2, n)), dma((2, n)), dma((2, n)), dma((2, n)),
            dma, dma,
            dma((nz,)), dma((nz,)), dma((nz,)), dma((nz,)),
        ],
        compiler_params=pltpu.CompilerParams(
            collective_id=0, has_side_effects=True, vmem_limit_bytes=60 * 2**20
        ),
        name="cox",
    )(
        dosages,
        coefficients.reshape(1, feats),
        directions,
        event_rank.reshape(rows // 128, 128),
        events.reshape(rows // 128, 128),
    )


def solution(mesh):
    nz, chips = mesh.shape["ex"], mesh.shape["feat"] // 2
    n = round(chips**0.5)
    placed = (P("ex", "feat"), P("feat"), P("feat", None), P("ex"), P("ex"))
    return jax.shard_map(
        functools.partial(local, nz, n), mesh=mesh, in_specs=placed, out_specs=P("feat", None), check_vma=False
    )
```

```python
import functools

import jax
import jax.numpy as jnp
from jax import lax
from jax.experimental import pallas as pl
from jax.experimental.pallas import tpu as pltpu
from jax.sharding import PartitionSpec as P

MESH = pl.DeviceIdType.MESH
F32 = jnp.float32
BF16 = jnp.bfloat16
LO = 256
STEPS = 32767.0


def row_of(tile):
    return jnp.concatenate([tile[i : i + 1, :] for i in range(tile.shape[0])], axis=1)


def split_pair(value):
    high = value.astype(BF16)
    return high, value - high.astype(F32)


def kernel(
    nz, n, d_hbm, coef_hbm, dirs_hbm, rank_hbm, ev_hbm, out_ref,
    rank_v, ev_v, dfull, d2, dirs2, coef_v, tsend, tcode, unit, runit, lin0, rlin0, lin1, recv1, rlin1,
    r2, lin2, recv2, rlin2, m1, hrep, hi8, lhs, lhr, t8s, risks, sel,
    zr1, zw, zc, zrc, zq, zrq, zu, zru, tot, abuf, pbuf, prec, ps, zr3, obuf,
    lsem, send, recv,
):
    rows = d_hbm.shape[0]
    half, sub, hi_n = rows // 2, rows // 4, rows // LO
    z, f = lax.axis_index("ex"), lax.axis_index("feat")
    c, chip = lax.rem(f, 2), lax.div(f, 2)
    x, y = lax.rem(chip, n), lax.div(chip, n)
    other = 1 - c

    def at(yy, xx, cc):
        return {"feat": (yy * n + xx) * 2 + cc}

    def along(zz, cc):
        return {"ex": zz, "feat": (y * n + x) * 2 + cc}

    partner = at(y, x, other)
    xs = [lax.rem(x + d, n) for d in range(n)]
    ys = [lax.rem(y + d, n) for d in range(n)]
    zs = [lax.rem(z + d, nz) for d in range(nz)]
    far = sorted(range(1, nz), key=lambda d: -min(d, nz - d))

    def remote(src, dst, send, recv, device):
        return pltpu.make_async_remote_copy(
            src_ref=src, dst_ref=dst, send_sem=send, recv_sem=recv,
            device_id=device, device_id_type=MESH,
        )

    def landed(view, k):
        remote(view, view, send.at[k], recv.at[k], partner).wait_recv()

    def left(view, k):
        remote(view, view, send.at[k], recv.at[k], partner).wait_send()

    barrier = pltpu.get_barrier_semaphore()
    for d in far:
        for cc in range(2):
            pl.semaphore_signal(barrier, inc=1, device_id=along(zs[d], cc), device_id_type=MESH)
    for d in range(1, n):
        for cc in range(2):
            pl.semaphore_signal(barrier, inc=1, device_id=at(ys[d], x, cc), device_id_type=MESH)
            pl.semaphore_signal(barrier, inc=1, device_id=at(y, xs[d], cc), device_id_type=MESH)
    pl.semaphore_signal(barrier, inc=1, device_id=partner, device_id_type=MESH)

    lanes = pl.ds(pl.multiple_of(c * 128, 128), 128)
    mine = pl.ds(pl.multiple_of(c * half, half), half)
    away = pl.ds(pl.multiple_of(other * half, half), half)
    own_full = pltpu.make_async_copy(d_hbm, dfull, lsem.at[0])
    own_coef = pltpu.make_async_copy(coef_hbm, coef_v, lsem.at[1])
    own_rank = pltpu.make_async_copy(rank_hbm, rank_v, lsem.at[2])
    own_dirs = pltpu.make_async_copy(dirs_hbm, dirs2.at[c], lsem.at[3])
    own_d = pltpu.make_async_copy(d_hbm.at[mine], d2.at[:, lanes], lsem.at[4])
    own_ev = pltpu.make_async_copy(ev_hbm, ev_v, lsem.at[5])
    for copy in (own_coef, own_full, own_rank, own_dirs, own_d, own_ev):
        copy.start()
    over_both = (((1,), (1,)), ((), ()))
    own_coef.wait()
    own_full.wait()
    slopes = jnp.broadcast_to(coef_v[...].astype(F32), (16, 128)).astype(BF16)
    lin0[...] = lax.dot_general(slopes, dfull[...], over_both, preferred_element_type=F32)[0:1]
    own_rank.wait()

    place = row_of(rank_v[...]) & (rows - 1)
    hi_b = jnp.broadcast_to(place >> 8, (8, rows))
    lo_b = jnp.broadcast_to(place & (LO - 1), (8, rows))
    hi8[...] = hi_b
    level = lax.broadcasted_iota(jnp.int32, (8, rows), 0)
    for block in range(LO // 16):
        upper = (lo_b >= level + block * 16).astype(F32)
        lower = (lo_b >= level + (block * 16 + 8)).astype(F32)
        m1[block * 16 : block * 16 + 16, :] = jnp.concatenate([upper, lower], 0).astype(BF16)
    for hi in range(hi_n):
        same = (hi_b == hi).astype(F32)
        hrep[hi] = jnp.concatenate([same, same], 0).astype(BF16)

    pl.semaphore_wait(barrier, 2 * (nz - 1) + 4 * (n - 1) + 1)

    swap_l = remote(lin0.at[:, away], rlin0, send.at[0], recv.at[0], partner)
    away_d = remote(d_hbm.at[away], d2.at[:, lanes], send.at[1], recv.at[1], partner)
    away_dirs = remote(dirs_hbm, dirs2.at[c], send.at[2], recv.at[2], partner)
    swap_l.start()
    away_d.start()
    away_dirs.start()
    own_dirs.wait()
    own_d.wait()
    swap_l.wait()
    lin1[...] = lin0[:, mine] + rlin0[...]
    for d in range(n - 1, 0, -1):
        remote(lin1, rlin1.at[d], send.at[3], recv.at[3], at(y, xs[d], c)).start()
    away_dirs.wait()
    away_d.wait()

    weights = jnp.concatenate(
        [dirs2[cc].astype(F32).T.astype(BF16) for cc in range(2)], axis=1
    )
    def code(part):
        people = d2[part * sub : part * sub + sub, :]
        tangent = lax.dot_general(weights, people, over_both, preferred_element_type=F32)
        tsend[part] = tangent.reshape(n, n, 8, sub)
        top = jnp.max(jnp.max(jnp.abs(tangent), axis=0, keepdims=True), axis=1, keepdims=True)
        top = jnp.maximum(top, 1e-30)
        level = jnp.floor(tangent * (STEPS / top) + 0.5).astype(jnp.int32).astype(jnp.int16)
        tcode[part] = level.reshape(n, n, 8, sub)
        unit[part] = jnp.broadcast_to(top * (1.0 / STEPS), (1, 128))

    def ship(part):
        for d in range(n - 1, 0, -1):
            if part == 0:
                source, device = tcode.at[0, xs[d]], at(y, xs[d], c)
            else:
                source, device = tcode.at[1, :, ys[d]], at(ys[d], x, c)
            remote(unit.at[part], runit.at[part * n + d], send.at[4], recv.at[4], device).start()
            remote(source, recv1.at[part, d], send.at[5 + part], recv.at[5 + part], device).start()

    code(0)
    ship(0)
    code(1)

    left(rlin1.at[pl.ds(1, n - 1)], 3)
    landed(rlin1.at[pl.ds(1, n - 1)], 3)
    line = lin1[...]
    for d in range(1, n):
        line = line + rlin1[d]
    lin2[...] = line
    rlin2[c * n] = line
    for d in range(n - 1, -1, -1):
        for cc in (c, other):
            if d > 0 or cc is other:
                remote(lin2, rlin2.at[c * n + d], send.at[7], recv.at[7], at(ys[d], x, cc)).start()
    ship(1)
    own_ev.wait()
    ev = row_of(ev_v[...]).astype(F32)
    high = lax.broadcasted_iota(jnp.int32, (hi_n, rows), 0)
    place_hi = jnp.concatenate([hi_b] * (hi_n // 8), 0) if hi_n >= 8 else hi_b[:hi_n]
    same = (place_hi == high).astype(F32)
    lhr[0:hi_n] = (same * jnp.broadcast_to(ev, (hi_n, rows))).astype(BF16)
    late = lax.dot_general(lhr[0:hi_n], m1[...], over_both, preferred_element_type=F32)
    lane = lax.broadcasted_iota(jnp.int32, (hi_n, LO), 1)
    happened = late - jnp.where(lane == LO - 1, 0.0, pltpu.roll(late, LO - 1, 1))
    count_own = jnp.sum(ev, axis=1, keepdims=True)
    left(rlin2.at[pl.ds(0, 2 * n - 1)], 7)
    landed(rlin2.at[pl.ds(0, 2 * n - 1)], 7)

    for cc in range(2):
        span = slice(cc * half, cc * half + half)
        line = rlin2[cc * n]
        for d in range(1, n):
            line = line + rlin2[cc * n + d]
        risk = jnp.exp(jnp.broadcast_to(line, (8, half)))
        risks[:, span] = risk
        high_part, low_part = split_pair(jnp.concatenate([risk] * (-(-hi_n // 8)), 0)[:hi_n])
        lhr[0:hi_n, span] = (same[:, span] * high_part.astype(F32)).astype(BF16)
        lhr[hi_n : 2 * hi_n, span] = (same[:, span] * low_part).astype(BF16)
    inside = lax.dot_general(lhr[...], m1[...], over_both, preferred_element_type=F32)
    inside_r = inside[:hi_n] + inside[hi_n:]

    wide = (hi_n, 128)
    lane_w = lax.broadcasted_iota(jnp.int32, wide, 1)
    hi_w = lax.broadcasted_iota(jnp.int32, wide, 0)

    def scan_hi(col, forward):
        row = jnp.sum(jnp.where(lane_w == hi_w, jnp.broadcast_to(col, wide), 0.0), axis=0, keepdims=True)
        kept = lane_w < hi_w if forward else lane_w > hi_w
        carried = jnp.sum(jnp.where(kept, jnp.broadcast_to(row, wide), 0.0), axis=1, keepdims=True)
        return carried, jnp.sum(row, axis=1, keepdims=True)

    carry_r, sum_r = scan_hi(inside_r[:, 0:1], False)
    lane1 = lax.broadcasted_iota(jnp.int32, (1, 128), 1)
    one = (1, 128)
    at_local = inside_r + carry_r
    coded = jnp.where(happened > 0.5, at_local, 3e38)
    zw[z] = jnp.where(c == 0, coded[:, :128], coded[:, 128:])
    zr1[z] = jnp.where(lane1 == 0, jnp.broadcast_to(sum_r, one), 0.0) + jnp.where(
        lane1 == 1, jnp.broadcast_to(count_own, one), 0.0
    )
    for d in far:
        remote(zr1.at[z], zr1.at[z], send.at[8], recv.at[8], along(zs[d], c)).start()
    for d in far:
        remote(zw.at[z], zw.at[z], send.at[9], recv.at[9], along(zs[d], c)).start()

    left(runit.at[pl.ds(0, 2 * n - 2)], 4)
    landed(runit.at[pl.ds(0, 2 * n - 2)], 4)
    for part in range(2):
        left(recv1.at[part, pl.ds(1, n - 1)], 5 + part)
        landed(recv1.at[part, pl.ds(1, n - 1)], 5 + part)
        total = tsend[0, x] if part == 0 else tsend[1, :, y]
        for d in range(1, n):
            scale = runit[part * n + d][:, 0:1].reshape(1, 1, 1)
            total = total + recv1[part, d].astype(jnp.int32).astype(F32) * scale
        r2[part] = total
        recv2[(part * 2 + c) * n] = r2[part, y if part == 0 else x]
        for d in range(n - 1, -1, -1):
            for cc in (c, other):
                if d == 0 and cc is c:
                    continue
                if part == 0:
                    source, device = r2.at[0, ys[d]], at(ys[d], x, cc)
                else:
                    source, device = r2.at[1, xs[d]], at(y, xs[d], cc)
                remote(source, recv2.at[(part * 2 + c) * n + d], send.at[10], recv.at[10], device).start()

    def over_persons(row):
        tall = jnp.broadcast_to(row, (8, half)) if row.shape[0] == 1 else row
        _, low = split_pair(tall)
        got = jnp.dot(
            jnp.concatenate([tall, low], 0).astype(BF16), d2[...], preferred_element_type=F32
        )
        return got[0:1] + got[8:9]

    got = over_persons(risks[:, mine])
    zq[0] = got[:, :128]
    zq[1] = got[:, 128:]
    zrq[c * nz + z] = jnp.where(c == 0, got[:, :128], got[:, 128:])
    for d in far + [0]:
        for cc in (c, other):
            if d > 0 or cc is other:
                remote(zq.at[cc], zrq.at[c * nz + z], send.at[11], recv.at[11], along(zs[d], cc)).start()

    left(recv2.at[pl.ds(0, 4 * n - 2)], 10)
    landed(recv2.at[pl.ds(0, 4 * n - 2)], 10)

    for cc in range(2):
        for part in range(2):
            span = slice((cc * 2 + part) * sub, (cc * 2 + part + 1) * sub)
            total = recv2[(part * 2 + cc) * n]
            for d in range(1, n):
                total = total + recv2[(part * 2 + cc) * n + d]
            t8s[:, span] = total
            moved = total * risks[:, span]
            _, low = split_pair(moved)
            pieces = jnp.concatenate([moved, low], 0).astype(BF16)
            for hi in range(hi_n):
                lhs[hi * 16 : hi * 16 + 16, span] = pieces * hrep[hi, :, span]
    inside = lax.dot_general(
        lhs[...], m1[...], over_both, preferred_element_type=F32
    ).reshape(hi_n, 16, LO)
    inside_t = inside[:, 0:8] + inside[:, 8:16]
    carry_t = [None] * hi_n
    sum_t = jnp.zeros((8, 1), F32)
    for hi in range(hi_n - 1, -1, -1):
        carry_t[hi] = sum_t
        sum_t = sum_t + inside_t[hi][:, 0:1]

    left(zr1.at[pl.ds(0, nz - 1)], 8)
    landed(zr1.at[pl.ds(0, nz - 1)], 8)
    own_later = jnp.zeros(one, F32)
    for zz in range(nz):
        own_later = own_later + jnp.where(zz > z, zr1[zz], 0.0)

    at_risk = at_local + own_later[:, 0:1]
    hazard = happened / at_risk
    slope = happened / (at_risk * at_risk)
    before_h, _ = scan_hi(jnp.sum(hazard, axis=1, keepdims=True), True)
    before_g, sum_g = scan_hi(jnp.sum(slope, axis=1, keepdims=True), True)

    run_t = jnp.zeros((8, 1), F32)
    before, rates = [], []
    for hi in range(hi_n):
        row_h = jnp.broadcast_to(hazard[hi : hi + 1], (4, LO))
        row_g = jnp.broadcast_to(slope[hi : hi + 1], (8, LO))
        hazard_t = (inside_t[hi] + carry_t[hi]) * row_g
        before.append(
            jnp.concatenate(
                [
                    run_t,
                    jnp.broadcast_to(before_h[hi : hi + 1], (4, 1)),
                    jnp.broadcast_to(before_g[hi : hi + 1], (4, 1)),
                ],
                0,
            )
        )
        rates += [hazard_t, row_h, row_g[0:4]]
        run_t = run_t + jnp.sum(hazard_t, axis=1, keepdims=True)

    rate, rate_low = split_pair(jnp.concatenate(rates, 0))
    rate_low = rate_low.astype(BF16)
    width = min(512, half)
    for chunk in range(half // width):
        begin = pl.multiple_of(c * half + chunk * width, width)
        member = m1[:, pl.ds(begin, width)]
        spread = jnp.dot(rate, member, preferred_element_type=F32) + jnp.dot(
            rate_low, member, preferred_element_type=F32
        )
        spot = hi8[:, pl.ds(begin, width)]
        spot = jnp.concatenate([spot, spot], 0)
        chosen = jnp.zeros((16, width), F32)
        for hi in range(hi_n):
            chosen = jnp.where(spot == hi, spread[hi * 16 : hi * 16 + 16] + before[hi], chosen)
        sel[:, chunk * width : (chunk + 1) * width] = chosen

    got = over_persons(risks[:, mine] * jnp.broadcast_to(sel[12:13, :], (8, half)))
    wide_g = jnp.broadcast_to(sum_g, one)
    zu[0] = jnp.concatenate([got[:, :128], wide_g], 1)
    zu[1] = jnp.concatenate([got[:, 128:], wide_g], 1)
    for d in far:
        for cc in (c, other):
            remote(zu.at[cc], zru.at[c * nz + z], send.at[12], recv.at[12], along(zs[d], cc)).start()
    lane8 = lax.broadcasted_iota(jnp.int32, (8, 128), 1)
    tot[x, y] = jnp.where(lane8 == 0, jnp.broadcast_to(sum_t, (8, 128)), jnp.broadcast_to(run_t, (8, 128)))

    left(zw.at[pl.ds(0, nz - 1)], 9)
    landed(zw.at[pl.ds(0, nz - 1)], 9)
    later = jnp.zeros(one, F32)
    past = jnp.zeros(wide, F32)
    for zz in range(nz - 1, -1, -1):
        past = past + jnp.where(zz < z, 1.0 / (zw[zz] + later[:, 0:1]), 0.0)
        later = later + zr1[zz]
    count = later[:, 1:2]
    past = jnp.sum(jnp.sum(past, axis=0, keepdims=True), axis=1, keepdims=True)
    zc[...] = jnp.broadcast_to(past, one)
    swap_c = remote(zc, zrc, send.at[13], recv.at[13], partner)
    swap_c.start()
    swap_c.wait()
    early_h = (zc[...] + zrc[...])[:, 0:1]

    for part in range(2):
        span = slice(part * sub, part * sub + sub)
        begin = pl.multiple_of(c * half + part * sub, sub)
        tangent, risk = t8s[:, pl.ds(begin, sub)], risks[:, pl.ds(begin, sub)]
        hazards = jnp.broadcast_to(sel[8:9, span] + early_h, (8, sub))
        abuf[part, x, y] = (risk * (tangent * hazards - sel[0:8, span])).astype(BF16)
        for d in range(n - 1, 0, -1):
            device = at(ys[d], x, c) if part == 0 else at(y, xs[d], c)
            slot = abuf.at[part, x, y]
            remote(slot, slot, send.at[14 + part], recv.at[14 + part], device).start()
            if part == 0:
                slot = tot.at[x, y]
                remote(slot, slot, send.at[16], recv.at[16], device).start()
    for part in range(2):
        view = abuf.at[part, 0, pl.ds(0, n - 1)]
        left(view, 14 + part)
        landed(view, 14 + part)
        if part == 0:
            left(tot.at[0, pl.ds(0, n - 1)], 16)
            landed(tot.at[0, pl.ds(0, n - 1)], 16)
        source = abuf.at[0, x] if part == 0 else abuf.at[1, :, y]
        for d in range(n - 1, 0, -1):
            device = at(y, xs[d], c) if part == 0 else at(ys[d], x, c)
            remote(source, source, send.at[17 + part], recv.at[17 + part], device).start()
            if part == 0:
                slot = tot.at[x]
                remote(slot, slot, send.at[19], recv.at[19], device).start()
    for part in range(2):
        view = abuf.at[part, pl.ds(0, n - 1)]
        left(view, 17 + part)
        landed(view, 17 + part)
    left(tot.at[pl.ds(0, n - 1)], 19)
    landed(tot.at[pl.ds(0, n - 1)], 19)

    k_n = n * n * 8
    product = jnp.zeros((k_n, 256), F32)
    for part in range(2):
        product = product + jnp.dot(
            abuf[part].reshape(k_n, sub), d2[part * sub : part * sub + sub, :],
            preferred_element_type=F32,
        )
    pbuf[0] = product[:, :128]
    pbuf[1] = product[:, 128:]
    swap = remote(pbuf.at[other], prec, send.at[20], recv.at[20], partner)
    swap.start()
    left(zrq.at[pl.ds(0, 2 * nz - 1)], 11)
    landed(zrq.at[pl.ds(0, 2 * nz - 1)], 11)
    left(zru.at[pl.ds(0, 2 * nz - 2)], 12)
    landed(zru.at[pl.ds(0, 2 * nz - 2)], 12)
    beyond = jnp.zeros(one, F32)
    before_u = jnp.zeros(one, F32)
    after_q = jnp.zeros(one, F32)
    for zz in range(nz - 1, -1, -1):
        risk_sum = zrq[zz] + zrq[nz + zz]
        slope_sum = zru[zz][:, :128] + zru[nz + zz][:, :128] + zru[zz][:, 128:] * beyond
        before_u = before_u + jnp.where(zz < z, slope_sum, 0.0)
        after_q = after_q + jnp.where(zz > z, risk_sum, 0.0)
        beyond = beyond + risk_sum
    totals = tot[...].reshape(k_n, 128)
    fixed = totals[:, 0:1] * before_u + totals[:, 1:2] * after_q
    swap.wait()
    share = k_n // nz
    ps[...] = (pbuf[c] + prec[...] - fixed).reshape(nz, share, 128)
    for d in far:
        remote(ps.at[zs[d]], zr3.at[d], send.at[21], recv.at[21], along(zs[d], c)).start()
    left(zr3.at[pl.ds(1, nz - 1)], 21)
    landed(zr3.at[pl.ds(1, nz - 1)], 21)
    done = ps[z]
    for d in range(1, nz):
        done = done + zr3[d]
    obuf[z] = done / count
    for d in far:
        remote(obuf.at[z], obuf.at[z], send.at[22], recv.at[22], along(zs[d], c)).start()
    left(obuf.at[pl.ds(0, nz - 1)], 22)
    landed(obuf.at[pl.ds(0, nz - 1)], 22)
    out_ref[...] = obuf[...].reshape(k_n, 128).T


def local(nz, n, dosages, coefficients, directions, event_rank, events):
    rows, feats = dosages.shape
    k_n = directions.shape[1]
    sub, half, hi_n = rows // 4, rows // 2, rows // LO
    vmem = pl.BlockSpec(memory_space=pltpu.VMEM)
    dma = pltpu.SemaphoreType.DMA
    return pl.pallas_call(
        functools.partial(kernel, nz, n),
        out_shape=jax.ShapeDtypeStruct((feats, k_n), F32),
        in_specs=[pl.BlockSpec(memory_space=pl.ANY)] * 5,
        out_specs=vmem,
        scratch_shapes=[
            pltpu.VMEM((rows // 128, 128), jnp.int32),
            pltpu.VMEM((rows // 128, 128), jnp.int32),
            pltpu.VMEM((rows, feats), BF16),
            pltpu.VMEM((half, 2 * feats), BF16),
            pltpu.VMEM((2, feats, k_n), BF16),
            pltpu.VMEM((1, feats), BF16),
            pltpu.VMEM((2, n, n, 8, sub), F32),
            pltpu.VMEM((2, n, n, 8, sub), jnp.int16),
            pltpu.VMEM((2, 1, 128), F32),
            pltpu.VMEM((2 * n, 1, 128), F32),
            pltpu.VMEM((1, rows), F32),
            pltpu.VMEM((1, half), F32),
            pltpu.VMEM((1, half), F32),
            pltpu.VMEM((2, n, n, 8, sub), jnp.int16),
            pltpu.VMEM((n, 1, half), F32),
            pltpu.VMEM((2, n, 8, sub), F32),
            pltpu.VMEM((1, half), F32),
            pltpu.VMEM((4 * n, 8, sub), F32),
            pltpu.VMEM((2 * n, 1, half), F32),
            pltpu.VMEM((LO, rows), BF16),
            pltpu.VMEM((hi_n, 16, rows), BF16),
            pltpu.VMEM((8, rows), jnp.int32),
            pltpu.VMEM((hi_n * 16, rows), BF16),
            pltpu.VMEM((hi_n * 2, rows), BF16),
            pltpu.VMEM((8, rows), F32),
            pltpu.VMEM((8, rows), F32),
            pltpu.VMEM((16, half), F32),
            pltpu.VMEM((nz, 1, 128), F32),
            pltpu.VMEM((nz, hi_n, 128), F32),
            pltpu.VMEM((1, 128), F32),
            pltpu.VMEM((1, 128), F32),
            pltpu.VMEM((2, 1, 128), F32),
            pltpu.VMEM((2 * nz, 1, 128), F32),
            pltpu.VMEM((2, 1, 256), F32),
            pltpu.VMEM((2 * nz, 1, 256), F32),
            pltpu.VMEM((n, n, 8, 128), F32),
            pltpu.VMEM((2, n, n, 8, sub), BF16),
            pltpu.VMEM((2, k_n, 128), F32),
            pltpu.VMEM((k_n, 128), F32),
            pltpu.VMEM((nz, k_n // nz, 128), F32),
            pltpu.VMEM((nz, k_n // nz, 128), F32),
            pltpu.VMEM((nz, k_n // nz, 128), F32),
            dma((6,)),
            dma((23,)),
            dma((23,)),
        ],
        compiler_params=pltpu.CompilerParams(
            collective_id=0, has_side_effects=True, vmem_limit_bytes=60 * 2**20
        ),
        name="cox",
    )(
        dosages,
        coefficients.reshape(1, feats),
        directions,
        event_rank.reshape(rows // 128, 128),
        events.reshape(rows // 128, 128),
    )


def solution(mesh):
    nz, chips = mesh.shape["ex"], mesh.shape["feat"] // 2
    n = round(chips**0.5)
    placed = (P("ex", "feat"), P("feat"), P("feat", None), P("ex"), P("ex"))
    return jax.shard_map(
        functools.partial(local, nz, n), mesh=mesh, in_specs=placed, out_specs=P("feat", None), check_vma=False
    )
```

```python
import functools

import jax
import jax.numpy as jnp
from jax import lax
from jax.experimental import pallas as pl
from jax.experimental.pallas import tpu as pltpu
from jax.sharding import PartitionSpec as P

MESH = pl.DeviceIdType.MESH
F32 = jnp.float32
BF16 = jnp.bfloat16
LO = 256
STEPS = 32767.0
VMEM_MIB = 30


def row_of(tile):
    return jnp.concatenate([tile[i : i + 1, :] for i in range(tile.shape[0])], axis=1)


def split_pair(value):
    high = value.astype(BF16)
    return high, value - high.astype(F32)


def kernel(
    nz, n, d_hbm, coef_hbm, dirs_hbm, rank_hbm, ev_hbm, out_ref,
    rank_v, ev_v, dfull, d2, dirs2, coef_v, tsend, tcode, unit, runit, lin0, rlin0, lin1, recv1, rlin1,
    r2, grain, rgrain, lin2, recv2, rlin2, m1, hrep, hi8, lhs, lhr, t8s, risks, sel,
    zr1, zw, zc, zrc, zq, zrq, zu, zru, tot, abuf, pbuf, prec, ps, zr3, obuf,
    lsem, send, recv,
):
    rows = d_hbm.shape[0]
    half, sub, hi_n = rows // 2, rows // 4, rows // LO
    z, f = lax.axis_index("ex"), lax.axis_index("feat")
    c, chip = lax.rem(f, 2), lax.div(f, 2)
    x, y = lax.rem(chip, n), lax.div(chip, n)
    other = 1 - c

    def at(yy, xx, cc):
        return {"feat": (yy * n + xx) * 2 + cc}

    def along(zz, cc):
        return {"ex": zz, "feat": (y * n + x) * 2 + cc}

    partner = at(y, x, other)
    xs = [lax.rem(x + d, n) for d in range(n)]
    ys = [lax.rem(y + d, n) for d in range(n)]
    zs = [lax.rem(z + d, nz) for d in range(nz)]
    far = sorted(range(1, nz), key=lambda d: -min(d, nz - d))

    def remote(src, dst, send, recv, device):
        return pltpu.make_async_remote_copy(
            src_ref=src, dst_ref=dst, send_sem=send, recv_sem=recv,
            device_id=device, device_id_type=MESH,
        )

    def landed(view, k):
        remote(view, view, send.at[k], recv.at[k], partner).wait_recv()

    def left(view, k):
        remote(view, view, send.at[k], recv.at[k], partner).wait_send()

    barrier = pltpu.get_barrier_semaphore()
    for d in far:
        for cc in range(2):
            pl.semaphore_signal(barrier, inc=1, device_id=along(zs[d], cc), device_id_type=MESH)
    for d in range(1, n):
        for cc in range(2):
            pl.semaphore_signal(barrier, inc=1, device_id=at(ys[d], x, cc), device_id_type=MESH)
            pl.semaphore_signal(barrier, inc=1, device_id=at(y, xs[d], cc), device_id_type=MESH)
    pl.semaphore_signal(barrier, inc=1, device_id=partner, device_id_type=MESH)

    lanes = pl.ds(pl.multiple_of(c * 128, 128), 128)
    mine = pl.ds(pl.multiple_of(c * half, half), half)
    away = pl.ds(pl.multiple_of(other * half, half), half)
    own_full = pltpu.make_async_copy(d_hbm, dfull, lsem.at[0])
    own_coef = pltpu.make_async_copy(coef_hbm, coef_v, lsem.at[1])
    own_rank = pltpu.make_async_copy(rank_hbm, rank_v, lsem.at[2])
    own_dirs = pltpu.make_async_copy(dirs_hbm, dirs2.at[c], lsem.at[3])
    own_d = pltpu.make_async_copy(d_hbm.at[mine], d2.at[:, lanes], lsem.at[4])
    own_ev = pltpu.make_async_copy(ev_hbm, ev_v, lsem.at[5])
    for copy in (own_coef, own_full, own_rank, own_dirs, own_d, own_ev):
        copy.start()
    over_both = (((1,), (1,)), ((), ()))
    own_coef.wait()
    own_full.wait()
    slopes = jnp.broadcast_to(coef_v[...].astype(F32), (16, 128)).astype(BF16)
    lin0[...] = lax.dot_general(slopes, dfull[...], over_both, preferred_element_type=F32)[0:1]
    own_rank.wait()
    pl.semaphore_wait(barrier, 2 * (nz - 1) + 4 * (n - 1) + 1)

    swap_l = remote(lin0.at[:, away], rlin0, send.at[0], recv.at[0], partner)
    away_d = remote(d_hbm.at[away], d2.at[:, lanes], send.at[1], recv.at[1], partner)
    away_dirs = remote(dirs_hbm, dirs2.at[c], send.at[2], recv.at[2], partner)
    swap_l.start()
    away_d.start()
    away_dirs.start()
    place = row_of(rank_v[...]) & (rows - 1)
    hi_b = jnp.broadcast_to(place >> 8, (8, rows))
    lo_b = jnp.broadcast_to(place & (LO - 1), (8, rows))
    hi8[...] = hi_b
    level = lax.broadcasted_iota(jnp.int32, (8, rows), 0)
    for block in range(LO // 16):
        upper = (lo_b >= level + block * 16).astype(F32)
        lower = (lo_b >= level + (block * 16 + 8)).astype(F32)
        m1[block * 16 : block * 16 + 16, :] = jnp.concatenate([upper, lower], 0).astype(BF16)
    for hi in range(hi_n):
        same = (hi_b == hi).astype(F32)
        hrep[hi] = jnp.concatenate([same, same], 0).astype(BF16)

    own_dirs.wait()
    own_d.wait()
    swap_l.wait()
    lin1[...] = lin0[:, mine] + rlin0[...]
    for d in range(n - 1, 0, -1):
        remote(lin1, rlin1.at[d], send.at[3], recv.at[3], at(y, xs[d], c)).start()
    away_dirs.wait()
    away_d.wait()

    weights = jnp.concatenate(
        [dirs2[cc].astype(F32).T.astype(BF16) for cc in range(2)], axis=1
    )
    def encode(value, shape):
        flat = value.reshape(-1, value.shape[-1])
        top = jnp.max(jnp.max(jnp.abs(flat), axis=0, keepdims=True), axis=1, keepdims=True)
        top = jnp.maximum(top, 1e-30)
        level = jnp.floor(flat * (STEPS / top) + 0.5).astype(jnp.int32).astype(jnp.int16)
        return level.reshape(shape), jnp.broadcast_to(top * (1.0 / STEPS), (1, 128))

    def code(part):
        people = d2[part * sub : part * sub + sub, :]
        tangent = lax.dot_general(weights, people, over_both, preferred_element_type=F32)
        tsend[part] = tangent.reshape(n, n, 8, sub)
        tcode[part], unit[part] = encode(tangent, (n, n, 8, sub))

    def ship(part):
        for d in range(n - 1, 0, -1):
            if part == 0:
                source, device = tcode.at[0, xs[d]], at(y, xs[d], c)
            else:
                source, device = tcode.at[1, :, ys[d]], at(ys[d], x, c)
            remote(unit.at[part], runit.at[part * n + d], send.at[4], recv.at[4], device).start()
            remote(source, recv1.at[part, d], send.at[5 + part], recv.at[5 + part], device).start()

    code(0)
    ship(0)
    code(1)

    left(rlin1.at[pl.ds(1, n - 1)], 3)
    landed(rlin1.at[pl.ds(1, n - 1)], 3)
    line = lin1[...]
    for d in range(1, n):
        line = line + rlin1[d]
    lin2[...] = line
    rlin2[c * n] = line
    for d in range(n - 1, -1, -1):
        for cc in (c, other):
            if d > 0 or cc is other:
                remote(lin2, rlin2.at[c * n + d], send.at[7], recv.at[7], at(ys[d], x, cc)).start()
    ship(1)
    own_ev.wait()
    ev = row_of(ev_v[...]).astype(F32)
    high = lax.broadcasted_iota(jnp.int32, (hi_n, rows), 0)
    place_hi = jnp.concatenate([hi_b] * (hi_n // 8), 0) if hi_n >= 8 else hi_b[:hi_n]
    same = (place_hi == high).astype(F32)
    lhr[0:hi_n] = (same * jnp.broadcast_to(ev, (hi_n, rows))).astype(BF16)
    late = lax.dot_general(lhr[0:hi_n], m1[...], over_both, preferred_element_type=F32)
    lane = lax.broadcasted_iota(jnp.int32, (hi_n, LO), 1)
    happened = late - jnp.where(lane == LO - 1, 0.0, pltpu.roll(late, LO - 1, 1))
    count_own = jnp.sum(ev, axis=1, keepdims=True)
    left(rlin2.at[pl.ds(0, 2 * n - 1)], 7)
    landed(rlin2.at[pl.ds(0, 2 * n - 1)], 7)

    lane1 = lax.broadcasted_iota(jnp.int32, (1, 128), 1)
    one = (1, 128)
    sum_r = jnp.zeros((1, 1), F32)
    for cc in range(2):
        line = rlin2[cc * n]
        for d in range(1, n):
            line = line + rlin2[cc * n + d]
        risk = jnp.exp(jnp.broadcast_to(line, (8, half)))
        risks[:, cc * half : cc * half + half] = risk
        sum_r = sum_r + jnp.sum(risk[0:1], axis=1, keepdims=True)
    zr1[z] = jnp.where(lane1 == 0, jnp.broadcast_to(sum_r, one), 0.0) + jnp.where(
        lane1 == 1, jnp.broadcast_to(count_own, one), 0.0
    )
    for d in far:
        remote(zr1.at[z], zr1.at[z], send.at[8], recv.at[8], along(zs[d], c)).start()
    for cc in range(2):
        span = slice(cc * half, cc * half + half)
        tall = jnp.concatenate([risks[:, span]] * (-(-hi_n // 8)), 0)[:hi_n]
        high_part, low_part = split_pair(tall)
        lhr[0:hi_n, span] = (same[:, span] * high_part.astype(F32)).astype(BF16)
        lhr[hi_n : 2 * hi_n, span] = (same[:, span] * low_part).astype(BF16)
    inside = lax.dot_general(lhr[...], m1[...], over_both, preferred_element_type=F32)
    inside_r = inside[:hi_n] + inside[hi_n:]

    wide = (hi_n, 128)
    lane_w = lax.broadcasted_iota(jnp.int32, wide, 1)
    hi_w = lax.broadcasted_iota(jnp.int32, wide, 0)

    def scan_hi(col, forward):
        row = jnp.sum(jnp.where(lane_w == hi_w, jnp.broadcast_to(col, wide), 0.0), axis=0, keepdims=True)
        kept = lane_w < hi_w if forward else lane_w > hi_w
        carried = jnp.sum(jnp.where(kept, jnp.broadcast_to(row, wide), 0.0), axis=1, keepdims=True)
        return carried, jnp.sum(row, axis=1, keepdims=True)

    carry_r, _ = scan_hi(inside_r[:, 0:1], False)
    at_local = inside_r + carry_r
    coded = jnp.where(happened > 0.5, jnp.minimum(at_local * (STEPS / sum_r), STEPS), -1.0)
    coded = jnp.where(c == 0, coded[:, :128], coded[:, 128:])
    zw[z] = jnp.floor(coded + 0.5).astype(jnp.int32).astype(jnp.int16)
    for d in far:
        remote(zw.at[z], zw.at[z], send.at[9], recv.at[9], along(zs[d], c)).start()

    left(runit.at[pl.ds(0, 2 * n - 2)], 4)
    landed(runit.at[pl.ds(0, 2 * n - 2)], 4)
    for part in range(2):
        left(recv1.at[part, pl.ds(1, n - 1)], 5 + part)
        landed(recv1.at[part, pl.ds(1, n - 1)], 5 + part)
        total = tsend[0, x] if part == 0 else tsend[1, :, y]
        for d in range(1, n):
            scale = runit[part * n + d][:, 0:1].reshape(1, 1, 1)
            total = total + recv1[part, d].astype(jnp.int32).astype(F32) * scale
        r2[part], grain[part] = encode(total, (n, 8, sub))
        recv2[(part * 2 + c) * n] = r2[part, y if part == 0 else x]
        rgrain[(part * 2 + c) * n] = grain[part]
        for d in range(n - 1, -1, -1):
            for cc in (c, other):
                if d == 0 and cc is c:
                    continue
                if part == 0:
                    source, device = r2.at[0, ys[d]], at(ys[d], x, cc)
                else:
                    source, device = r2.at[1, xs[d]], at(y, xs[d], cc)
                spot = (part * 2 + c) * n + d
                remote(grain.at[part], rgrain.at[spot], send.at[23], recv.at[23], device).start()
                remote(source, recv2.at[spot], send.at[10], recv.at[10], device).start()

    def over_persons(row):
        tall = jnp.broadcast_to(row, (8, half)) if row.shape[0] == 1 else row
        _, low = split_pair(tall)
        got = jnp.dot(
            jnp.concatenate([tall, low], 0).astype(BF16), d2[...], preferred_element_type=F32
        )
        return got[0:1] + got[8:9]

    got = over_persons(risks[:, mine])
    zq[0] = got[:, :128]
    zq[1] = got[:, 128:]
    zrq[c * nz + z] = jnp.where(c == 0, got[:, :128], got[:, 128:])
    for d in far + [0]:
        for cc in (c, other):
            if d > 0 or cc is other:
                remote(zq.at[cc], zrq.at[c * nz + z], send.at[11], recv.at[11], along(zs[d], cc)).start()

    left(recv2.at[pl.ds(0, 4 * n - 2)], 10)
    landed(recv2.at[pl.ds(0, 4 * n - 2)], 10)
    left(rgrain.at[pl.ds(0, 4 * n - 2)], 23)
    landed(rgrain.at[pl.ds(0, 4 * n - 2)], 23)

    for cc in range(2):
        for part in range(2):
            span = slice((cc * 2 + part) * sub, (cc * 2 + part + 1) * sub)
            total = jnp.zeros((8, sub), F32)
            for d in range(n):
                spot = (part * 2 + cc) * n + d
                total = total + recv2[spot].astype(jnp.int32).astype(F32) * rgrain[spot][:, 0:1]
            t8s[:, span] = total
            moved = total * risks[:, span]
            _, low = split_pair(moved)
            pieces = jnp.concatenate([moved, low], 0).astype(BF16)
            for hi in range(hi_n):
                lhs[hi * 16 : hi * 16 + 16, span] = pieces * hrep[hi, :, span]
    inside = lax.dot_general(
        lhs[...], m1[...], over_both, preferred_element_type=F32
    ).reshape(hi_n, 16, LO)
    inside_t = inside[:, 0:8] + inside[:, 8:16]
    carry_t = [None] * hi_n
    sum_t = jnp.zeros((8, 1), F32)
    for hi in range(hi_n - 1, -1, -1):
        carry_t[hi] = sum_t
        sum_t = sum_t + inside_t[hi][:, 0:1]

    left(zr1.at[pl.ds(0, nz - 1)], 8)
    landed(zr1.at[pl.ds(0, nz - 1)], 8)
    own_later = jnp.zeros(one, F32)
    for zz in range(nz):
        own_later = own_later + jnp.where(zz > z, zr1[zz], 0.0)

    at_risk = at_local + own_later[:, 0:1]
    hazard = happened / at_risk
    slope = happened / (at_risk * at_risk)
    before_h, _ = scan_hi(jnp.sum(hazard, axis=1, keepdims=True), True)
    before_g, sum_g = scan_hi(jnp.sum(slope, axis=1, keepdims=True), True)

    run_t = jnp.zeros((8, 1), F32)
    before, rates = [], []
    for hi in range(hi_n):
        row_h = jnp.broadcast_to(hazard[hi : hi + 1], (4, LO))
        row_g = jnp.broadcast_to(slope[hi : hi + 1], (8, LO))
        hazard_t = (inside_t[hi] + carry_t[hi]) * row_g
        before.append(
            jnp.concatenate(
                [
                    run_t,
                    jnp.broadcast_to(before_h[hi : hi + 1], (4, 1)),
                    jnp.broadcast_to(before_g[hi : hi + 1], (4, 1)),
                ],
                0,
            )
        )
        rates += [hazard_t, row_h, row_g[0:4]]
        run_t = run_t + jnp.sum(hazard_t, axis=1, keepdims=True)

    def exchange_past():
        left(zw.at[pl.ds(0, nz - 1)], 9)
        landed(zw.at[pl.ds(0, nz - 1)], 9)
        later = jnp.zeros(one, F32)
        past = jnp.zeros(wide, F32)
        for zz in range(nz - 1, -1, -1):
            level = zw[zz].astype(jnp.int32).astype(F32)
            share = 1.0 / (level * (zr1[zz][:, 0:1] * (1.0 / STEPS)) + later[:, 0:1])
            past = past + jnp.where(level >= 0.0, jnp.where(zz < z, share, 0.0), 0.0)
            later = later + zr1[zz]
        count = later[:, 1:2]
        past = jnp.sum(jnp.sum(past, axis=0, keepdims=True), axis=1, keepdims=True)
        zc[...] = jnp.broadcast_to(past, one)
        swap_c = remote(zc, zrc, send.at[13], recv.at[13], partner)
        swap_c.start()
        return swap_c, count

    rate, rate_low = split_pair(jnp.concatenate(rates, 0))
    rate_low = rate_low.astype(BF16)
    width = min(512, half)
    for chunk in range(half // width):
        if chunk == half // width // 2:
            swap_c, count = exchange_past()
        begin = pl.multiple_of(c * half + chunk * width, width)
        member = m1[:, pl.ds(begin, width)]
        spread = jnp.dot(rate, member, preferred_element_type=F32) + jnp.dot(
            rate_low, member, preferred_element_type=F32
        )
        spot = hi8[:, pl.ds(begin, width)]
        spot = jnp.concatenate([spot, spot], 0)
        chosen = jnp.zeros((16, width), F32)
        for hi in range(hi_n):
            chosen = jnp.where(spot == hi, spread[hi * 16 : hi * 16 + 16] + before[hi], chosen)
        sel[:, chunk * width : (chunk + 1) * width] = chosen

    lane8 = lax.broadcasted_iota(jnp.int32, (8, 128), 1)

    swap_c.wait()
    early_h = (zc[...] + zrc[...])[:, 0:1]

    tops = []
    for part in range(2):
        span = slice(part * sub, part * sub + sub)
        begin = pl.multiple_of(c * half + part * sub, sub)
        tangent, risk = t8s[:, pl.ds(begin, sub)], risks[:, pl.ds(begin, sub)]
        hazards = jnp.broadcast_to(sel[8:9, span] + early_h, (8, sub))
        weighted = risk * (tangent * hazards - sel[0:8, span])
        top = jnp.maximum(jnp.max(jnp.abs(weighted), axis=1, keepdims=True), 1e-30)
        abuf[part, x, y] = jnp.floor(weighted * (STEPS / top) + 0.5).astype(jnp.int32).astype(jnp.int16)
        tops.append(top * (1.0 / STEPS))
    columns = [sum_t, run_t] + tops
    tile = jnp.broadcast_to(columns[3], (8, 128))
    for place_k in range(3):
        tile = jnp.where(lane8 == place_k, jnp.broadcast_to(columns[place_k], (8, 128)), tile)
    tot[x, y] = tile
    for part in range(2):
        for d in range(n - 1, 0, -1):
            device = at(ys[d], x, c) if part == 0 else at(y, xs[d], c)
            slot = abuf.at[part, x, y]
            remote(slot, slot, send.at[14 + part], recv.at[14 + part], device).start()
            if part == 0:
                slot = tot.at[x, y]
                remote(slot, slot, send.at[16], recv.at[16], device).start()
    got = over_persons(risks[:, mine] * jnp.broadcast_to(sel[12:13, :], (8, half)))
    wide_g = jnp.broadcast_to(sum_g, one)
    zu[0] = jnp.concatenate([got[:, :128], wide_g], 1)
    zu[1] = jnp.concatenate([got[:, 128:], wide_g], 1)
    for d in far:
        for cc in (c, other):
            remote(zu.at[cc], zru.at[c * nz + z], send.at[12], recv.at[12], along(zs[d], cc)).start()
    for part in range(2):
        view = abuf.at[part, 0, pl.ds(0, n - 1)]
        left(view, 14 + part)
        landed(view, 14 + part)
        if part == 0:
            left(tot.at[0, pl.ds(0, n - 1)], 16)
            landed(tot.at[0, pl.ds(0, n - 1)], 16)
        source = abuf.at[0, x] if part == 0 else abuf.at[1, :, y]
        for d in range(n - 1, 0, -1):
            device = at(y, xs[d], c) if part == 0 else at(ys[d], x, c)
            remote(source, source, send.at[17 + part], recv.at[17 + part], device).start()
            if part == 0:
                slot = tot.at[x]
                remote(slot, slot, send.at[19], recv.at[19], device).start()
    for part in range(2):
        view = abuf.at[part, pl.ds(0, n - 1)]
        left(view, 17 + part)
        landed(view, 17 + part)
    left(tot.at[pl.ds(0, n - 1)], 19)
    landed(tot.at[pl.ds(0, n - 1)], 19)

    k_n = n * n * 8
    totals = tot[...].reshape(k_n, 128)
    digits = []
    for part in range(2):
        level = abuf[part].reshape(k_n, sub).astype(jnp.int32)
        upper = (level >> 8).astype(F32).astype(BF16)
        lower = (level & 255).astype(F32).astype(BF16)
        digits.append((upper, lower))

    def multiply(columns_d):
        product = jnp.zeros((k_n, 128), F32)
        for part in range(2):
            people = d2[part * sub : part * sub + sub, columns_d]
            upper = jnp.dot(digits[part][0], people, preferred_element_type=F32)
            lower = jnp.dot(digits[part][1], people, preferred_element_type=F32)
            product = product + (upper * 256.0 + lower) * totals[:, 2 + part : 3 + part]
        return product

    pbuf[0] = multiply(pl.ds(pl.multiple_of(other * 128, 128), 128))
    swap = remote(pbuf.at[0], prec, send.at[20], recv.at[20], partner)
    swap.start()
    product = multiply(lanes)
    left(zrq.at[pl.ds(0, 2 * nz - 1)], 11)
    landed(zrq.at[pl.ds(0, 2 * nz - 1)], 11)
    left(zru.at[pl.ds(0, 2 * nz - 2)], 12)
    landed(zru.at[pl.ds(0, 2 * nz - 2)], 12)
    beyond = jnp.zeros(one, F32)
    before_u = jnp.zeros(one, F32)
    after_q = jnp.zeros(one, F32)
    for zz in range(nz - 1, -1, -1):
        risk_sum = zrq[zz] + zrq[nz + zz]
        slope_sum = zru[zz][:, :128] + zru[nz + zz][:, :128] + zru[zz][:, 128:] * beyond
        before_u = before_u + jnp.where(zz < z, slope_sum, 0.0)
        after_q = after_q + jnp.where(zz > z, risk_sum, 0.0)
        beyond = beyond + risk_sum
    fixed = totals[:, 0:1] * before_u + totals[:, 1:2] * after_q
    swap.wait()
    share = k_n // nz
    ps[...] = (product + prec[...] - fixed).reshape(nz, share, 128)
    for d in far:
        remote(ps.at[zs[d]], zr3.at[d], send.at[21], recv.at[21], along(zs[d], c)).start()
    left(zr3.at[pl.ds(1, nz - 1)], 21)
    landed(zr3.at[pl.ds(1, nz - 1)], 21)
    done = ps[z]
    for d in range(1, nz):
        done = done + zr3[d]
    obuf[z] = done / count
    for d in far:
        remote(obuf.at[z], obuf.at[z], send.at[22], recv.at[22], along(zs[d], c)).start()
    left(obuf.at[pl.ds(0, nz - 1)], 22)
    landed(obuf.at[pl.ds(0, nz - 1)], 22)
    out_ref[...] = obuf[...].reshape(k_n, 128).T


def local(nz, n, dosages, coefficients, directions, event_rank, events):
    rows, feats = dosages.shape
    k_n = directions.shape[1]
    sub, half, hi_n = rows // 4, rows // 2, rows // LO
    vmem = pl.BlockSpec(memory_space=pltpu.VMEM)
    dma = pltpu.SemaphoreType.DMA
    return pl.pallas_call(
        functools.partial(kernel, nz, n),
        out_shape=jax.ShapeDtypeStruct((feats, k_n), F32),
        in_specs=[pl.BlockSpec(memory_space=pltpu.HBM)] * 5,
        out_specs=vmem,
        scratch_shapes=[
            pltpu.VMEM((rows // 128, 128), jnp.int32),
            pltpu.VMEM((rows // 128, 128), jnp.int32),
            pltpu.VMEM((rows, feats), BF16),
            pltpu.VMEM((half, 2 * feats), BF16),
            pltpu.VMEM((2, feats, k_n), BF16),
            pltpu.VMEM((1, feats), BF16),
            pltpu.VMEM((2, n, n, 8, sub), F32),
            pltpu.VMEM((2, n, n, 8, sub), jnp.int16),
            pltpu.VMEM((2, 1, 128), F32),
            pltpu.VMEM((2 * n, 1, 128), F32),
            pltpu.VMEM((1, rows), F32),
            pltpu.VMEM((1, half), F32),
            pltpu.VMEM((1, half), F32),
            pltpu.VMEM((2, n, n, 8, sub), jnp.int16),
            pltpu.VMEM((n, 1, half), F32),
            pltpu.VMEM((2, n, 8, sub), jnp.int16),
            pltpu.VMEM((2, 1, 128), F32),
            pltpu.VMEM((4 * n, 1, 128), F32),
            pltpu.VMEM((1, half), F32),
            pltpu.VMEM((4 * n, 8, sub), jnp.int16),
            pltpu.VMEM((2 * n, 1, half), F32),
            pltpu.VMEM((LO, rows), BF16),
            pltpu.VMEM((hi_n, 16, rows), BF16),
            pltpu.VMEM((8, rows), jnp.int32),
            pltpu.VMEM((hi_n * 16, rows), BF16),
            pltpu.VMEM((hi_n * 2, rows), BF16),
            pltpu.VMEM((8, rows), F32),
            pltpu.VMEM((8, rows), F32),
            pltpu.VMEM((16, half), F32),
            pltpu.VMEM((nz, 1, 128), F32),
            pltpu.VMEM((nz, hi_n, 128), jnp.int16),
            pltpu.VMEM((1, 128), F32),
            pltpu.VMEM((1, 128), F32),
            pltpu.VMEM((2, 1, 128), F32),
            pltpu.VMEM((2 * nz, 1, 128), F32),
            pltpu.VMEM((2, 1, 256), F32),
            pltpu.VMEM((2 * nz, 1, 256), F32),
            pltpu.VMEM((n, n, 8, 128), F32),
            pltpu.VMEM((2, n, n, 8, sub), jnp.int16),
            pltpu.VMEM((1, k_n, 128), F32),
            pltpu.VMEM((k_n, 128), F32),
            pltpu.VMEM((nz, k_n // nz, 128), F32),
            pltpu.VMEM((nz, k_n // nz, 128), F32),
            pltpu.VMEM((nz, k_n // nz, 128), F32),
            dma((6,)),
            dma((24,)),
            dma((24,)),
        ],
        compiler_params=pltpu.CompilerParams(
            collective_id=0, has_side_effects=True, vmem_limit_bytes=VMEM_MIB * 2**20
        ),
        name="cox",
    )(
        *(
            pltpu.with_memory_space_constraint(a, pltpu.HBM)
            for a in (
                dosages,
                coefficients.reshape(1, feats),
                directions,
                event_rank.reshape(rows // 128, 128),
                events.reshape(rows // 128, 128),
            )
        )
    )


def solution(mesh):
    nz, chips = mesh.shape["ex"], mesh.shape["feat"] // 2
    n = round(chips**0.5)
    placed = (P("ex", "feat"), P("feat"), P("feat", None), P("ex"), P("ex"))
    return jax.shard_map(
        functools.partial(local, nz, n), mesh=mesh, in_specs=placed, out_specs=P("feat", None), check_vma=False
    )
```

```python
import functools

import jax
import jax.numpy as jnp
from jax import lax
from jax.experimental import pallas as pl
from jax.experimental.pallas import tpu as pltpu
from jax.sharding import PartitionSpec as P

MESH = pl.DeviceIdType.MESH
F32 = jnp.float32
BF16 = jnp.bfloat16
LO = 256
STEPS = 32767.0
VMEM_MIB = 30


def row_of(tile):
    return jnp.concatenate([tile[i : i + 1, :] for i in range(tile.shape[0])], axis=1)


def split_pair(value):
    high = value.astype(BF16)
    return high, value - high.astype(F32)


def kernel(
    nz, n, d_hbm, coef_hbm, dirs_hbm, rank_hbm, ev_hbm, out_ref,
    rank_v, ev_v, dfull, d2, dirs2, coef_v, tsend, tcode, unit, runit, lin0, rlin0, lin1, recv1, rlin1,
    r2, grain, rgrain, lin2, recv2, rlin2, m1, hrep, hi8, lhs, lhr, t8s, risks, sel,
    zr1, zw, zc, zrc, zq, zrq, zu, zru, tot, abuf, pbuf, prec, ps, pu, zr3, zr3u, obuf,
    lsem, send, recv, recv_at,
):
    rows = d_hbm.shape[0]
    half, sub, hi_n = rows // 2, rows // 4, rows // LO
    z, f = lax.axis_index("ex"), lax.axis_index("feat")
    c, chip = lax.rem(f, 2), lax.div(f, 2)
    x, y = lax.rem(chip, n), lax.div(chip, n)
    other = 1 - c

    def at(yy, xx, cc):
        return {"feat": (yy * n + xx) * 2 + cc}

    def along(zz, cc):
        return {"ex": zz, "feat": (y * n + x) * 2 + cc}

    partner = at(y, x, other)
    xs = [lax.rem(x + d, n) for d in range(n)]
    ys = [lax.rem(y + d, n) for d in range(n)]
    zs = [lax.rem(z + d, nz) for d in range(nz)]
    far = sorted(range(1, nz), key=lambda d: -min(d, nz - d))

    def remote(src, dst, send, recv, device):
        return pltpu.make_async_remote_copy(
            src_ref=src, dst_ref=dst, send_sem=send, recv_sem=recv,
            device_id=device, device_id_type=MESH,
        )

    def landed(view, k):
        remote(view, view, send.at[k], recv.at[k], partner).wait_recv()

    def left(view, k):
        remote(view, view, send.at[k], recv.at[k], partner).wait_send()

    barrier = pltpu.get_barrier_semaphore()
    for d in far:
        for cc in range(2):
            pl.semaphore_signal(barrier, inc=1, device_id=along(zs[d], cc), device_id_type=MESH)
    for d in range(1, n):
        for cc in range(2):
            pl.semaphore_signal(barrier, inc=1, device_id=at(ys[d], x, cc), device_id_type=MESH)
            pl.semaphore_signal(barrier, inc=1, device_id=at(y, xs[d], cc), device_id_type=MESH)
    pl.semaphore_signal(barrier, inc=1, device_id=partner, device_id_type=MESH)

    lanes = pl.ds(pl.multiple_of(c * 128, 128), 128)
    mine = pl.ds(pl.multiple_of(c * half, half), half)
    away = pl.ds(pl.multiple_of(other * half, half), half)
    own_full = pltpu.make_async_copy(d_hbm, dfull, lsem.at[0])
    own_coef = pltpu.make_async_copy(coef_hbm, coef_v, lsem.at[1])
    own_rank = pltpu.make_async_copy(rank_hbm, rank_v, lsem.at[2])
    own_dirs = pltpu.make_async_copy(dirs_hbm, dirs2.at[c], lsem.at[3])
    own_d = pltpu.make_async_copy(d_hbm.at[mine], d2.at[:, lanes], lsem.at[4])
    own_ev = pltpu.make_async_copy(ev_hbm, ev_v, lsem.at[5])
    for copy in (own_coef, own_full, own_rank, own_dirs, own_d, own_ev):
        copy.start()
    over_both = (((1,), (1,)), ((), ()))
    own_coef.wait()
    own_full.wait()
    slopes = jnp.broadcast_to(coef_v[...].astype(F32), (16, 128)).astype(BF16)
    lin0[...] = lax.dot_general(slopes, dfull[...], over_both, preferred_element_type=F32)[0:1]
    own_rank.wait()
    pl.semaphore_wait(barrier, 2 * (nz - 1) + 4 * (n - 1) + 1)

    swap_l = remote(lin0.at[:, away], rlin0, send.at[0], recv.at[0], partner)
    away_d = remote(d_hbm.at[away], d2.at[:, lanes], send.at[1], recv.at[1], partner)
    away_dirs = remote(dirs_hbm, dirs2.at[c], send.at[2], recv.at[2], partner)
    swap_l.start()
    away_d.start()
    away_dirs.start()
    place = row_of(rank_v[...]) & (rows - 1)
    hi_b = jnp.broadcast_to(place >> 8, (8, rows))
    lo_b = jnp.broadcast_to(place & (LO - 1), (8, rows))
    hi8[...] = hi_b
    level = lax.broadcasted_iota(jnp.int32, (8, rows), 0)
    for block in range(LO // 16):
        upper = (lo_b >= level + block * 16).astype(F32)
        lower = (lo_b >= level + (block * 16 + 8)).astype(F32)
        m1[block * 16 : block * 16 + 16, :] = jnp.concatenate([upper, lower], 0).astype(BF16)
    for hi in range(hi_n):
        same = (hi_b == hi).astype(F32)
        hrep[hi] = jnp.concatenate([same, same], 0).astype(BF16)

    own_dirs.wait()
    own_d.wait()
    swap_l.wait()
    lin1[...] = lin0[:, mine] + rlin0[...]
    for d in range(n - 1, 0, -1):
        remote(lin1, rlin1.at[d], send.at[3], recv.at[3], at(y, xs[d], c)).start()
    away_dirs.wait()
    away_d.wait()

    weights = jnp.concatenate(
        [dirs2[cc].astype(F32).T.astype(BF16) for cc in range(2)], axis=1
    )
    def encode(value, shape):
        flat = value.reshape(-1, value.shape[-1])
        top = jnp.max(jnp.max(jnp.abs(flat), axis=0, keepdims=True), axis=1, keepdims=True)
        top = jnp.maximum(top, 1e-30)
        level = jnp.floor(flat * (STEPS / top) + 0.5).astype(jnp.int32).astype(jnp.int16)
        return level.reshape(shape), jnp.broadcast_to(top * (1.0 / STEPS), (1, 128))

    def code(part):
        people = d2[part * sub : part * sub + sub, :]
        tangent = lax.dot_general(weights, people, over_both, preferred_element_type=F32)
        tsend[part] = tangent.reshape(n, n, 8, sub)
        tcode[part], unit[part] = encode(tangent, (n, n, 8, sub))

    def ship(part):
        for d in range(n - 1, 0, -1):
            if part == 0:
                source, device = tcode.at[0, xs[d]], at(y, xs[d], c)
            else:
                source, device = tcode.at[1, :, ys[d]], at(ys[d], x, c)
            remote(unit.at[part], runit.at[part * n + d], send.at[4], recv.at[4], device).start()
            remote(source, recv1.at[part, d], send.at[5 + part], recv.at[5 + part], device).start()

    code(0)
    ship(0)
    code(1)

    left(rlin1.at[pl.ds(1, n - 1)], 3)
    landed(rlin1.at[pl.ds(1, n - 1)], 3)
    line = lin1[...]
    for d in range(1, n):
        line = line + rlin1[d]
    lin2[...] = line
    rlin2[c * n] = line
    for d in range(n - 1, -1, -1):
        for cc in (c, other):
            if d > 0 or cc is other:
                remote(lin2, rlin2.at[c * n + d], send.at[7], recv.at[7], at(ys[d], x, cc)).start()
    ship(1)
    own_ev.wait()
    ev = row_of(ev_v[...]).astype(F32)
    high = lax.broadcasted_iota(jnp.int32, (hi_n, rows), 0)
    place_hi = jnp.concatenate([hi_b] * (hi_n // 8), 0) if hi_n >= 8 else hi_b[:hi_n]
    same = (place_hi == high).astype(F32)
    lhr[0:hi_n] = (same * jnp.broadcast_to(ev, (hi_n, rows))).astype(BF16)
    late = lax.dot_general(lhr[0:hi_n], m1[...], over_both, preferred_element_type=F32)
    lane = lax.broadcasted_iota(jnp.int32, (hi_n, LO), 1)
    happened = late - jnp.where(lane == LO - 1, 0.0, pltpu.roll(late, LO - 1, 1))
    count_own = jnp.sum(ev, axis=1, keepdims=True)
    left(rlin2.at[pl.ds(0, 2 * n - 1)], 7)
    landed(rlin2.at[pl.ds(0, 2 * n - 1)], 7)

    lane1 = lax.broadcasted_iota(jnp.int32, (1, 128), 1)
    one = (1, 128)
    sum_r = jnp.zeros((1, 1), F32)
    for cc in range(2):
        line = rlin2[cc * n]
        for d in range(1, n):
            line = line + rlin2[cc * n + d]
        risk = jnp.exp(jnp.broadcast_to(line, (8, half)))
        risks[:, cc * half : cc * half + half] = risk
        sum_r = sum_r + jnp.sum(risk[0:1], axis=1, keepdims=True)
    zr1[z] = jnp.where(lane1 == 0, jnp.broadcast_to(sum_r, one), 0.0) + jnp.where(
        lane1 == 1, jnp.broadcast_to(count_own, one), 0.0
    )
    for d in far:
        remote(zr1.at[z], zr1.at[z], send.at[8], recv.at[8], along(zs[d], c)).start()
    for cc in range(2):
        span = slice(cc * half, cc * half + half)
        tall = jnp.concatenate([risks[:, span]] * (-(-hi_n // 8)), 0)[:hi_n]
        high_part, low_part = split_pair(tall)
        lhr[0:hi_n, span] = (same[:, span] * high_part.astype(F32)).astype(BF16)
        lhr[hi_n : 2 * hi_n, span] = (same[:, span] * low_part).astype(BF16)
    inside = lax.dot_general(lhr[...], m1[...], over_both, preferred_element_type=F32)
    inside_r = inside[:hi_n] + inside[hi_n:]

    wide = (hi_n, 128)
    lane_w = lax.broadcasted_iota(jnp.int32, wide, 1)
    hi_w = lax.broadcasted_iota(jnp.int32, wide, 0)

    def scan_hi(col, forward):
        row = jnp.sum(jnp.where(lane_w == hi_w, jnp.broadcast_to(col, wide), 0.0), axis=0, keepdims=True)
        kept = lane_w < hi_w if forward else lane_w > hi_w
        carried = jnp.sum(jnp.where(kept, jnp.broadcast_to(row, wide), 0.0), axis=1, keepdims=True)
        return carried, jnp.sum(row, axis=1, keepdims=True)

    carry_r, _ = scan_hi(inside_r[:, 0:1], False)
    at_local = inside_r + carry_r
    coded = jnp.where(happened > 0.5, jnp.minimum(at_local * (STEPS / sum_r), STEPS), -1.0)
    coded = jnp.where(c == 0, coded[:, :128], coded[:, 128:])
    zw[z] = jnp.floor(coded + 0.5).astype(jnp.int32).astype(jnp.int16)
    for d in far:
        remote(zw.at[z], zw.at[z], send.at[9], recv.at[9], along(zs[d], c)).start()

    left(runit.at[pl.ds(0, 2 * n - 2)], 4)
    landed(runit.at[pl.ds(0, 2 * n - 2)], 4)
    for part in range(2):
        left(recv1.at[part, pl.ds(1, n - 1)], 5 + part)
        landed(recv1.at[part, pl.ds(1, n - 1)], 5 + part)
        total = tsend[0, x] if part == 0 else tsend[1, :, y]
        for d in range(1, n):
            scale = runit[part * n + d][:, 0:1].reshape(1, 1, 1)
            total = total + recv1[part, d].astype(jnp.int32).astype(F32) * scale
        r2[part], grain[part] = encode(total, (n, 8, sub))
        recv2[(part * 2 + c) * n] = r2[part, y if part == 0 else x]
        rgrain[(part * 2 + c) * n] = grain[part]
        for d in range(n - 1, -1, -1):
            for cc in (c, other):
                if d == 0 and cc is c:
                    continue
                if part == 0:
                    source, device = r2.at[0, ys[d]], at(ys[d], x, cc)
                else:
                    source, device = r2.at[1, xs[d]], at(y, xs[d], cc)
                spot = (part * 2 + c) * n + d
                remote(grain.at[part], rgrain.at[spot], send.at[23], recv.at[23], device).start()
                remote(source, recv2.at[spot], send.at[10], recv.at[10], device).start()

    def over_persons(row):
        tall = jnp.broadcast_to(row, (8, half)) if row.shape[0] == 1 else row
        _, low = split_pair(tall)
        got = jnp.dot(
            jnp.concatenate([tall, low], 0).astype(BF16), d2[...], preferred_element_type=F32
        )
        return got[0:1] + got[8:9]

    got = over_persons(risks[:, mine])
    zq[0] = got[:, :128]
    zq[1] = got[:, 128:]
    zrq[c * nz + z] = jnp.where(c == 0, got[:, :128], got[:, 128:])
    for d in far + [0]:
        for cc in (c, other):
            if d > 0 or cc is other:
                remote(zq.at[cc], zrq.at[c * nz + z], send.at[11], recv.at[11], along(zs[d], cc)).start()

    left(recv2.at[pl.ds(0, 4 * n - 2)], 10)
    landed(recv2.at[pl.ds(0, 4 * n - 2)], 10)
    left(rgrain.at[pl.ds(0, 4 * n - 2)], 23)
    landed(rgrain.at[pl.ds(0, 4 * n - 2)], 23)

    for cc in range(2):
        for part in range(2):
            span = slice((cc * 2 + part) * sub, (cc * 2 + part + 1) * sub)
            total = jnp.zeros((8, sub), F32)
            for d in range(n):
                spot = (part * 2 + cc) * n + d
                total = total + recv2[spot].astype(jnp.int32).astype(F32) * rgrain[spot][:, 0:1]
            t8s[:, span] = total
            moved = total * risks[:, span]
            _, low = split_pair(moved)
            pieces = jnp.concatenate([moved, low], 0).astype(BF16)
            for hi in range(hi_n):
                lhs[hi * 16 : hi * 16 + 16, span] = pieces * hrep[hi, :, span]
    inside = lax.dot_general(
        lhs[...], m1[...], over_both, preferred_element_type=F32
    ).reshape(hi_n, 16, LO)
    inside_t = inside[:, 0:8] + inside[:, 8:16]
    carry_t = [None] * hi_n
    sum_t = jnp.zeros((8, 1), F32)
    for hi in range(hi_n - 1, -1, -1):
        carry_t[hi] = sum_t
        sum_t = sum_t + inside_t[hi][:, 0:1]

    left(zr1.at[pl.ds(0, nz - 1)], 8)
    landed(zr1.at[pl.ds(0, nz - 1)], 8)
    own_later = jnp.zeros(one, F32)
    for zz in range(nz):
        own_later = own_later + jnp.where(zz > z, zr1[zz], 0.0)

    at_risk = at_local + own_later[:, 0:1]
    hazard = happened / at_risk
    slope = happened / (at_risk * at_risk)
    before_h, _ = scan_hi(jnp.sum(hazard, axis=1, keepdims=True), True)
    before_g, sum_g = scan_hi(jnp.sum(slope, axis=1, keepdims=True), True)

    run_t = jnp.zeros((8, 1), F32)
    before, rates = [], []
    for hi in range(hi_n):
        row_h = jnp.broadcast_to(hazard[hi : hi + 1], (4, LO))
        row_g = jnp.broadcast_to(slope[hi : hi + 1], (8, LO))
        hazard_t = (inside_t[hi] + carry_t[hi]) * row_g
        before.append(
            jnp.concatenate(
                [
                    run_t,
                    jnp.broadcast_to(before_h[hi : hi + 1], (4, 1)),
                    jnp.broadcast_to(before_g[hi : hi + 1], (4, 1)),
                ],
                0,
            )
        )
        rates += [hazard_t, row_h, row_g[0:4]]
        run_t = run_t + jnp.sum(hazard_t, axis=1, keepdims=True)

    def exchange_past():
        left(zw.at[pl.ds(0, nz - 1)], 9)
        landed(zw.at[pl.ds(0, nz - 1)], 9)
        later = jnp.zeros(one, F32)
        past = jnp.zeros(wide, F32)
        for zz in range(nz - 1, -1, -1):
            level = zw[zz].astype(jnp.int32).astype(F32)
            share = 1.0 / (level * (zr1[zz][:, 0:1] * (1.0 / STEPS)) + later[:, 0:1])
            past = past + jnp.where(level >= 0.0, jnp.where(zz < z, share, 0.0), 0.0)
            later = later + zr1[zz]
        count = later[:, 1:2]
        past = jnp.sum(jnp.sum(past, axis=0, keepdims=True), axis=1, keepdims=True)
        zc[...] = jnp.broadcast_to(past, one)
        swap_c = remote(zc, zrc, send.at[13], recv.at[13], partner)
        swap_c.start()
        return swap_c, count

    rate, rate_low = split_pair(jnp.concatenate(rates, 0))
    rate_low = rate_low.astype(BF16)
    width = min(512, half)
    for chunk in range(half // width):
        if chunk == half // width // 2:
            swap_c, count = exchange_past()
        begin = pl.multiple_of(c * half + chunk * width, width)
        member = m1[:, pl.ds(begin, width)]
        spread = jnp.dot(rate, member, preferred_element_type=F32) + jnp.dot(
            rate_low, member, preferred_element_type=F32
        )
        spot = hi8[:, pl.ds(begin, width)]
        spot = jnp.concatenate([spot, spot], 0)
        chosen = jnp.zeros((16, width), F32)
        for hi in range(hi_n):
            chosen = jnp.where(spot == hi, spread[hi * 16 : hi * 16 + 16] + before[hi], chosen)
        sel[:, chunk * width : (chunk + 1) * width] = chosen

    lane8 = lax.broadcasted_iota(jnp.int32, (8, 128), 1)

    swap_c.wait()
    early_h = (zc[...] + zrc[...])[:, 0:1]

    tops = []
    for part in range(2):
        span = slice(part * sub, part * sub + sub)
        begin = pl.multiple_of(c * half + part * sub, sub)
        tangent, risk = t8s[:, pl.ds(begin, sub)], risks[:, pl.ds(begin, sub)]
        hazards = jnp.broadcast_to(sel[8:9, span] + early_h, (8, sub))
        weighted = risk * (tangent * hazards - sel[0:8, span])
        top = jnp.maximum(jnp.max(jnp.abs(weighted), axis=1, keepdims=True), 1e-30)
        abuf[part, x, y] = jnp.floor(weighted * (STEPS / top) + 0.5).astype(jnp.int32).astype(jnp.int16)
        tops.append(top * (1.0 / STEPS))
    columns = [sum_t, run_t] + tops
    tile = jnp.broadcast_to(columns[3], (8, 128))
    for place_k in range(3):
        tile = jnp.where(lane8 == place_k, jnp.broadcast_to(columns[place_k], (8, 128)), tile)
    tot[x, y] = tile

    def cross(part, slot_of, k, turn):
        for d in turn:
            device = at(y, xs[d], c) if part == 0 else at(ys[d], x, c)
            for ref, sem in ((abuf.at[part], k),) + (((tot, 19),) if part == 0 else ()):
                remote(slot_of(ref), slot_of(ref), send.at[sem], recv.at[sem], device).start()

    turn = sorted(range(1, n), key=lambda d: -min(d, n - d))
    nearest = turn[::-1]
    for part in range(2):
        for d in turn:
            device = at(ys[d], x, c) if part == 0 else at(y, xs[d], c)
            for ref, sem in ((abuf.at[part], 14 + part),) + (((tot, 16),) if part == 0 else ()):
                slot = ref.at[x, y]
                arrive = recv_at.at[(part if sem < 16 else 2) * n + d]
                remote(slot, slot, send.at[sem], arrive, device).start()
    for part in range(2):
        cross(part, lambda ref: ref.at[x, y], 17 + part, turn)
    got = over_persons(risks[:, mine] * jnp.broadcast_to(sel[12:13, :], (8, half)))
    wide_g = jnp.broadcast_to(sum_g, one)
    zu[0] = jnp.concatenate([got[:, :128], wide_g], 1)
    zu[1] = jnp.concatenate([got[:, 128:], wide_g], 1)
    for d in far:
        for cc in (c, other):
            remote(zu.at[cc], zru.at[c * nz + z], send.at[12], recv.at[12], along(zs[d], cc)).start()
    for d in nearest:
        for part in range(2):
            if part == 0:
                spot = (x, lax.rem(y + n - d, n))
            else:
                spot = (lax.rem(x + n - d, n), y)
            for ref, row in ((abuf.at[part], part),) + (((tot, 2),) if part == 0 else ()):
                slot = ref.at[spot[0], spot[1]]
                remote(slot, slot, send.at[14], recv_at.at[row * n + d], partner).wait_recv()
            cross(part, lambda ref: ref.at[spot[0], spot[1]], 17 + part, turn)
    for part in range(2):
        left(abuf.at[part, 0, pl.ds(0, n - 1)], 14 + part)
    left(tot.at[0, pl.ds(0, n - 1)], 16)
    for part in range(2):
        view = abuf.at[part, pl.ds(0, n - 1)]
        left(view, 17 + part)
        landed(view, 17 + part)
    left(tot.at[pl.ds(0, n - 1)], 19)
    landed(tot.at[pl.ds(0, n - 1)], 19)

    k_n = n * n * 8
    totals = tot[...].reshape(k_n, 128)
    digits = []
    for part in range(2):
        level = abuf[part].reshape(k_n, sub).astype(jnp.int32)
        upper = (level >> 8).astype(F32).astype(BF16)
        lower = (level & 255).astype(F32).astype(BF16)
        digits.append((upper, lower))

    def multiply(columns_d):
        product = jnp.zeros((k_n, 128), F32)
        for part in range(2):
            people = d2[part * sub : part * sub + sub, columns_d]
            upper = jnp.dot(digits[part][0], people, preferred_element_type=F32)
            lower = jnp.dot(digits[part][1], people, preferred_element_type=F32)
            product = product + (upper * 256.0 + lower) * totals[:, 2 + part : 3 + part]
        return product

    pbuf[0] = multiply(pl.ds(pl.multiple_of(other * 128, 128), 128))
    swap = remote(pbuf.at[0], prec, send.at[20], recv.at[20], partner)
    swap.start()
    product = multiply(lanes)
    left(zrq.at[pl.ds(0, 2 * nz - 1)], 11)
    landed(zrq.at[pl.ds(0, 2 * nz - 1)], 11)
    left(zru.at[pl.ds(0, 2 * nz - 2)], 12)
    landed(zru.at[pl.ds(0, 2 * nz - 2)], 12)
    beyond = jnp.zeros(one, F32)
    before_u = jnp.zeros(one, F32)
    after_q = jnp.zeros(one, F32)
    for zz in range(nz - 1, -1, -1):
        risk_sum = zrq[zz] + zrq[nz + zz]
        slope_sum = zru[zz][:, :128] + zru[nz + zz][:, :128] + zru[zz][:, 128:] * beyond
        before_u = before_u + jnp.where(zz < z, slope_sum, 0.0)
        after_q = after_q + jnp.where(zz > z, risk_sum, 0.0)
        beyond = beyond + risk_sum
    fixed = totals[:, 0:1] * before_u + totals[:, 1:2] * after_q
    swap.wait()
    blocks = nz // 2
    share = k_n // blocks
    mine_b = lax.rem(z, blocks)
    total = (product + prec[...] - fixed).reshape(blocks, share, 128)
    top = jnp.max(jnp.max(jnp.abs(total), axis=1, keepdims=True), axis=2, keepdims=True)
    top = jnp.maximum(top, 1e-30)
    ps[...] = jnp.floor(total * (STEPS / top) + 0.5).astype(jnp.int32).astype(jnp.int16)
    pu[...] = jnp.broadcast_to(top * (1.0 / STEPS), (blocks, 1, 128))
    zr3[z] = ps[mine_b]
    zr3u[z] = pu[mine_b]
    for d in far:
        block = lax.rem(zs[d], blocks)
        remote(pu.at[block], zr3u.at[z], send.at[24], recv.at[24], along(zs[d], c)).start()
        remote(ps.at[block], zr3.at[z], send.at[21], recv.at[21], along(zs[d], c)).start()
    left(zr3.at[pl.ds(0, nz - 1)], 21)
    landed(zr3.at[pl.ds(0, nz - 1)], 21)
    left(zr3u.at[pl.ds(0, nz - 1)], 24)
    landed(zr3u.at[pl.ds(0, nz - 1)], 24)
    done = jnp.zeros((share, 128), F32)
    for zz in range(nz):
        done = done + zr3[zz].astype(jnp.int32).astype(F32) * zr3u[zz]
    obuf[mine_b] = done / count
    near = [d for d in far if d <= blocks // 2 or nz - d < blocks // 2]
    for d in near:
        slot = obuf.at[mine_b]
        remote(slot, slot, send.at[22], recv.at[22], along(zs[d], c)).start()
    if len(near) > 0:
        left(obuf.at[pl.ds(0, blocks - 1)], 22)
        landed(obuf.at[pl.ds(0, blocks - 1)], 22)
    out_ref[...] = obuf[...].reshape(k_n, 128).T


def local(nz, n, dosages, coefficients, directions, event_rank, events):
    rows, feats = dosages.shape
    k_n = directions.shape[1]
    sub, half, hi_n = rows // 4, rows // 2, rows // LO
    vmem = pl.BlockSpec(memory_space=pltpu.VMEM)
    dma = pltpu.SemaphoreType.DMA
    return pl.pallas_call(
        functools.partial(kernel, nz, n),
        out_shape=jax.ShapeDtypeStruct((feats, k_n), F32),
        in_specs=[pl.BlockSpec(memory_space=pltpu.HBM)] * 5,
        out_specs=vmem,
        scratch_shapes=[
            pltpu.VMEM((rows // 128, 128), jnp.int32),
            pltpu.VMEM((rows // 128, 128), jnp.int32),
            pltpu.VMEM((rows, feats), BF16),
            pltpu.VMEM((half, 2 * feats), BF16),
            pltpu.VMEM((2, feats, k_n), BF16),
            pltpu.VMEM((1, feats), BF16),
            pltpu.VMEM((2, n, n, 8, sub), F32),
            pltpu.VMEM((2, n, n, 8, sub), jnp.int16),
            pltpu.VMEM((2, 1, 128), F32),
            pltpu.VMEM((2 * n, 1, 128), F32),
            pltpu.VMEM((1, rows), F32),
            pltpu.VMEM((1, half), F32),
            pltpu.VMEM((1, half), F32),
            pltpu.VMEM((2, n, n, 8, sub), jnp.int16),
            pltpu.VMEM((n, 1, half), F32),
            pltpu.VMEM((2, n, 8, sub), jnp.int16),
            pltpu.VMEM((2, 1, 128), F32),
            pltpu.VMEM((4 * n, 1, 128), F32),
            pltpu.VMEM((1, half), F32),
            pltpu.VMEM((4 * n, 8, sub), jnp.int16),
            pltpu.VMEM((2 * n, 1, half), F32),
            pltpu.VMEM((LO, rows), BF16),
            pltpu.VMEM((hi_n, 16, rows), BF16),
            pltpu.VMEM((8, rows), jnp.int32),
            pltpu.VMEM((hi_n * 16, rows), BF16),
            pltpu.VMEM((hi_n * 2, rows), BF16),
            pltpu.VMEM((8, rows), F32),
            pltpu.VMEM((8, rows), F32),
            pltpu.VMEM((16, half), F32),
            pltpu.VMEM((nz, 1, 128), F32),
            pltpu.VMEM((nz, hi_n, 128), jnp.int16),
            pltpu.VMEM((1, 128), F32),
            pltpu.VMEM((1, 128), F32),
            pltpu.VMEM((2, 1, 128), F32),
            pltpu.VMEM((2 * nz, 1, 128), F32),
            pltpu.VMEM((2, 1, 256), F32),
            pltpu.VMEM((2 * nz, 1, 256), F32),
            pltpu.VMEM((n, n, 8, 128), F32),
            pltpu.VMEM((2, n, n, 8, sub), jnp.int16),
            pltpu.VMEM((1, k_n, 128), F32),
            pltpu.VMEM((k_n, 128), F32),
            pltpu.VMEM((nz // 2, k_n * 2 // nz, 128), jnp.int16),
            pltpu.VMEM((nz // 2, 1, 128), F32),
            pltpu.VMEM((nz, k_n * 2 // nz, 128), jnp.int16),
            pltpu.VMEM((nz, 1, 128), F32),
            pltpu.VMEM((nz // 2, k_n * 2 // nz, 128), F32),
            dma((6,)),
            dma((25,)),
            dma((25,)),
            dma((3 * n,)),
        ],
        compiler_params=pltpu.CompilerParams(
            collective_id=0, has_side_effects=True, vmem_limit_bytes=VMEM_MIB * 2**20
        ),
        name="cox",
    )(
        *(
            pltpu.with_memory_space_constraint(a, pltpu.HBM)
            for a in (
                dosages,
                coefficients.reshape(1, feats),
                directions,
                event_rank.reshape(rows // 128, 128),
                events.reshape(rows // 128, 128),
            )
        )
    )


def solution(mesh):
    nz, chips = mesh.shape["ex"], mesh.shape["feat"] // 2
    n = round(chips**0.5)
    placed = (P("ex", "feat"), P("feat"), P("feat", None), P("ex"), P("ex"))
    return jax.shard_map(
        functools.partial(local, nz, n), mesh=mesh, in_specs=placed, out_specs=P("feat", None), check_vma=False
    )
```

```python
import functools

import jax
import jax.numpy as jnp
from jax import lax
from jax.experimental import pallas as pl
from jax.experimental.pallas import tpu as pltpu
from jax.sharding import PartitionSpec as P

MESH = pl.DeviceIdType.MESH
F32 = jnp.float32
BF16 = jnp.bfloat16
LO = 256
STEPS = 32767.0
VMEM_MIB = 30


def row_of(tile):
    return jnp.concatenate([tile[i : i + 1, :] for i in range(tile.shape[0])], axis=1)


def split_pair(value):
    high = value.astype(BF16)
    return high, value - high.astype(F32)


def kernel(
    nz, n, d_hbm, coef_hbm, dirs_hbm, rank_hbm, ev_hbm, out_ref,
    rank_v, ev_v, dfull, d2, dirs2, coef_v, tsend, tcode, unit, runit, lin0, rlin0, lin1, recv1, rlin1,
    r2, grain, rgrain, lin2, recv2, rlin2, m1, hrep, hi8, lhs, lhr, t8s, risks, sel,
    zr1, zw, zc, zrc, zq, zrq, zu, zru, tot, abuf, pbuf, prec, ps, pu, zr3, zr3u, obuf,
    lsem, send, recv, recv_at,
):
    rows = d_hbm.shape[0]
    half, sub, hi_n = rows // 2, rows // 4, rows // LO
    z, f = lax.axis_index("ex"), lax.axis_index("feat")
    c, chip = lax.rem(f, 2), lax.div(f, 2)
    x, y = lax.rem(chip, n), lax.div(chip, n)
    other = 1 - c

    def at(yy, xx, cc):
        return {"feat": (yy * n + xx) * 2 + cc}

    def along(zz, cc):
        return {"ex": zz, "feat": (y * n + x) * 2 + cc}

    partner = at(y, x, other)
    xs = [lax.rem(x + d, n) for d in range(n)]
    ys = [lax.rem(y + d, n) for d in range(n)]
    zs = [lax.rem(z + d, nz) for d in range(nz)]
    far = sorted(range(1, nz), key=lambda d: -min(d, nz - d))
    turn = sorted(range(1, n), key=lambda d: -min(d, n - d))

    def remote(src, dst, send, recv, device):
        return pltpu.make_async_remote_copy(
            src_ref=src, dst_ref=dst, send_sem=send, recv_sem=recv,
            device_id=device, device_id_type=MESH,
        )

    def landed(view, k):
        remote(view, view, send.at[k], recv.at[k], partner).wait_recv()

    def left(view, k):
        remote(view, view, send.at[k], recv.at[k], partner).wait_send()

    barrier = pltpu.get_barrier_semaphore()
    for d in far:
        for cc in range(2):
            pl.semaphore_signal(barrier, inc=1, device_id=along(zs[d], cc), device_id_type=MESH)
    for d in range(1, n):
        for cc in range(2):
            pl.semaphore_signal(barrier, inc=1, device_id=at(ys[d], x, cc), device_id_type=MESH)
            pl.semaphore_signal(barrier, inc=1, device_id=at(y, xs[d], cc), device_id_type=MESH)
    pl.semaphore_signal(barrier, inc=1, device_id=partner, device_id_type=MESH)

    lanes = pl.ds(pl.multiple_of(c * 128, 128), 128)
    mine = pl.ds(pl.multiple_of(c * half, half), half)
    away = pl.ds(pl.multiple_of(other * half, half), half)
    own_full = pltpu.make_async_copy(d_hbm, dfull, lsem.at[0])
    own_coef = pltpu.make_async_copy(coef_hbm, coef_v, lsem.at[1])
    own_rank = pltpu.make_async_copy(rank_hbm, rank_v, lsem.at[2])
    own_dirs = pltpu.make_async_copy(dirs_hbm, dirs2.at[c], lsem.at[3])
    own_d = pltpu.make_async_copy(d_hbm.at[mine], d2.at[:, lanes], lsem.at[4])
    own_ev = pltpu.make_async_copy(ev_hbm, ev_v, lsem.at[5])
    for copy in (own_coef, own_full, own_rank, own_dirs, own_d, own_ev):
        copy.start()
    over_both = (((1,), (1,)), ((), ()))
    own_coef.wait()
    own_full.wait()
    slopes = jnp.broadcast_to(coef_v[...].astype(F32), (16, 128)).astype(BF16)
    lin0[...] = lax.dot_general(slopes, dfull[...], over_both, preferred_element_type=F32)[0:1]
    own_rank.wait()
    pl.semaphore_wait(barrier, 2 * (nz - 1) + 4 * (n - 1) + 1)

    swap_l = remote(lin0.at[:, away], rlin0, send.at[0], recv.at[0], partner)
    away_d = remote(d_hbm.at[away], d2.at[:, lanes], send.at[1], recv.at[1], partner)
    away_dirs = remote(dirs_hbm, dirs2.at[c], send.at[2], recv.at[2], partner)
    swap_l.start()
    away_d.start()
    away_dirs.start()
    place = row_of(rank_v[...]) & (rows - 1)
    hi_b = jnp.broadcast_to(place >> 8, (8, rows))
    lo_b = jnp.broadcast_to(place & (LO - 1), (8, rows))
    hi8[...] = hi_b
    level = lax.broadcasted_iota(jnp.int32, (8, rows), 0)
    for block in range(LO // 16):
        upper = (lo_b >= level + block * 16).astype(F32)
        lower = (lo_b >= level + (block * 16 + 8)).astype(F32)
        m1[block * 16 : block * 16 + 16, :] = jnp.concatenate([upper, lower], 0).astype(BF16)
    for hi in range(hi_n):
        same = (hi_b == hi).astype(F32)
        hrep[hi] = jnp.concatenate([same, same], 0).astype(BF16)

    own_dirs.wait()
    own_d.wait()
    swap_l.wait()
    lin1[...] = lin0[:, mine] + rlin0[...]
    for d in turn:
        remote(lin1, rlin1.at[d], send.at[3], recv.at[3], at(y, xs[d], c)).start()
    away_dirs.wait()
    away_d.wait()

    weights = jnp.concatenate(
        [dirs2[cc].astype(F32).T.astype(BF16) for cc in range(2)], axis=1
    )
    def encode(value, shape):
        flat = value.reshape(-1, value.shape[-1])
        top = jnp.max(jnp.max(jnp.abs(flat), axis=0, keepdims=True), axis=1, keepdims=True)
        top = jnp.maximum(top, 1e-30)
        level = jnp.floor(flat * (STEPS / top) + 0.5).astype(jnp.int32).astype(jnp.int16)
        return level.reshape(shape), jnp.broadcast_to(top * (1.0 / STEPS), (1, 128))

    def code(part):
        people = d2[part * sub : part * sub + sub, :]
        tangent = lax.dot_general(weights, people, over_both, preferred_element_type=F32)
        tsend[part] = tangent.reshape(n, n, 8, sub)
        tcode[part], unit[part] = encode(tangent, (n, n, 8, sub))

    def ship(part):
        for d in turn:
            if part == 0:
                source, device = tcode.at[0, xs[d]], at(y, xs[d], c)
            else:
                source, device = tcode.at[1, :, ys[d]], at(ys[d], x, c)
            remote(unit.at[part], runit.at[part * n + d], send.at[4], recv.at[4], device).start()
            remote(source, recv1.at[part, d], send.at[5 + part], recv.at[5 + part], device).start()

    code(0)
    ship(0)
    code(1)

    left(rlin1.at[pl.ds(1, n - 1)], 3)
    landed(rlin1.at[pl.ds(1, n - 1)], 3)
    line = lin1[...]
    for d in range(1, n):
        line = line + rlin1[d]
    lin2[...] = line
    rlin2[c * n] = line
    for d in turn + [0]:
        for cc in (c, other):
            if d > 0 or cc is other:
                remote(lin2, rlin2.at[c * n + d], send.at[7], recv.at[7], at(ys[d], x, cc)).start()
    ship(1)
    own_ev.wait()
    ev = row_of(ev_v[...]).astype(F32)
    high = lax.broadcasted_iota(jnp.int32, (hi_n, rows), 0)
    place_hi = jnp.concatenate([hi_b] * (hi_n // 8), 0) if hi_n >= 8 else hi_b[:hi_n]
    same = (place_hi == high).astype(F32)
    lhr[0:hi_n] = (same * jnp.broadcast_to(ev, (hi_n, rows))).astype(BF16)
    late = lax.dot_general(lhr[0:hi_n], m1[...], over_both, preferred_element_type=F32)
    lane = lax.broadcasted_iota(jnp.int32, (hi_n, LO), 1)
    happened = late - jnp.where(lane == LO - 1, 0.0, pltpu.roll(late, LO - 1, 1))
    count_own = jnp.sum(ev, axis=1, keepdims=True)
    left(rlin2.at[pl.ds(0, 2 * n - 1)], 7)
    landed(rlin2.at[pl.ds(0, 2 * n - 1)], 7)

    lane1 = lax.broadcasted_iota(jnp.int32, (1, 128), 1)
    one = (1, 128)
    sum_r = jnp.zeros((1, 1), F32)
    for cc in range(2):
        line = rlin2[cc * n]
        for d in range(1, n):
            line = line + rlin2[cc * n + d]
        risk = jnp.exp(jnp.broadcast_to(line, (8, half)))
        risks[:, cc * half : cc * half + half] = risk
        sum_r = sum_r + jnp.sum(risk[0:1], axis=1, keepdims=True)
    zr1[z] = jnp.where(lane1 == 0, jnp.broadcast_to(sum_r, one), 0.0) + jnp.where(
        lane1 == 1, jnp.broadcast_to(count_own, one), 0.0
    )
    for d in far:
        remote(zr1.at[z], zr1.at[z], send.at[8], recv.at[8], along(zs[d], c)).start()
    per_hi = jnp.zeros((hi_n, 1), F32)
    for cc in range(2):
        span = slice(cc * half, cc * half + half)
        tall = jnp.concatenate([risks[:, span]] * (-(-hi_n // 8)), 0)[:hi_n]
        per_hi = per_hi + jnp.sum(same[:, span] * tall, axis=1, keepdims=True)
        high_part, low_part = split_pair(tall)
        lhr[0:hi_n, span] = (same[:, span] * high_part.astype(F32)).astype(BF16)
        lhr[hi_n : 2 * hi_n, span] = (same[:, span] * low_part).astype(BF16)

    def risk_scan(core):
        some = m1[pl.ds(pl.multiple_of(core * 128, 128), 128), :]
        got = lax.dot_general(lhr[...], some, over_both, preferred_element_type=F32)
        return got[:hi_n] + got[hi_n:]

    wide = (hi_n, 128)
    lane_w = lax.broadcasted_iota(jnp.int32, wide, 1)
    hi_w = lax.broadcasted_iota(jnp.int32, wide, 0)

    def scan_hi(col, forward):
        row = jnp.sum(jnp.where(lane_w == hi_w, jnp.broadcast_to(col, wide), 0.0), axis=0, keepdims=True)
        kept = lane_w < hi_w if forward else lane_w > hi_w
        carried = jnp.sum(jnp.where(kept, jnp.broadcast_to(row, wide), 0.0), axis=1, keepdims=True)
        return carried, jnp.sum(row, axis=1, keepdims=True)

    carry_r, _ = scan_hi(per_hi, False)
    own_scan = risk_scan(c) + carry_r
    own_event = jnp.where(c == 0, happened[:, :128], happened[:, 128:])
    coded = jnp.where(own_event > 0.5, jnp.minimum(own_scan * (STEPS / sum_r), STEPS), -1.0)
    zw[z] = jnp.floor(coded + 0.5).astype(jnp.int32).astype(jnp.int16)
    for d in far:
        remote(zw.at[z], zw.at[z], send.at[9], recv.at[9], along(zs[d], c)).start()

    left(runit.at[pl.ds(0, 2 * n - 2)], 4)
    landed(runit.at[pl.ds(0, 2 * n - 2)], 4)
    for part in range(2):
        left(recv1.at[part, pl.ds(1, n - 1)], 5 + part)
        landed(recv1.at[part, pl.ds(1, n - 1)], 5 + part)
        total = tsend[0, x] if part == 0 else tsend[1, :, y]
        for d in range(1, n):
            scale = runit[part * n + d][:, 0:1].reshape(1, 1, 1)
            total = total + recv1[part, d].astype(jnp.int32).astype(F32) * scale
        r2[part], grain[part] = encode(total, (n, 8, sub))
        recv2[(part * 2 + c) * n] = r2[part, y if part == 0 else x]
        rgrain[(part * 2 + c) * n] = grain[part]
        for d in turn + [0]:
            for cc in (c, other):
                if d == 0 and cc is c:
                    continue
                if part == 0:
                    source, device = r2.at[0, ys[d]], at(ys[d], x, cc)
                else:
                    source, device = r2.at[1, xs[d]], at(y, xs[d], cc)
                spot = (part * 2 + c) * n + d
                remote(grain.at[part], rgrain.at[spot], send.at[23], recv.at[23], device).start()
                remote(source, recv2.at[spot], send.at[10], recv.at[10], device).start()

    other_scan = risk_scan(other) + carry_r
    at_local = jnp.concatenate(
        [jnp.where(c == 0, own_scan, other_scan), jnp.where(c == 0, other_scan, own_scan)], 1
    )
    def over_persons(row):
        tall = jnp.broadcast_to(row, (8, half)) if row.shape[0] == 1 else row
        _, low = split_pair(tall)
        got = jnp.dot(
            jnp.concatenate([tall, low], 0).astype(BF16), d2[...], preferred_element_type=F32
        )
        return got[0:1] + got[8:9]

    got = over_persons(risks[:, mine])
    zq[0] = got[:, :128]
    zq[1] = got[:, 128:]
    zrq[c * nz + z] = jnp.where(c == 0, got[:, :128], got[:, 128:])
    for d in far + [0]:
        for cc in (c, other):
            if d > 0 or cc is other:
                remote(zq.at[cc], zrq.at[c * nz + z], send.at[11], recv.at[11], along(zs[d], cc)).start()

    left(recv2.at[pl.ds(0, 4 * n - 2)], 10)
    landed(recv2.at[pl.ds(0, 4 * n - 2)], 10)
    left(rgrain.at[pl.ds(0, 4 * n - 2)], 23)
    landed(rgrain.at[pl.ds(0, 4 * n - 2)], 23)

    for cc in range(2):
        for part in range(2):
            span = slice((cc * 2 + part) * sub, (cc * 2 + part + 1) * sub)
            total = jnp.zeros((8, sub), F32)
            for d in range(n):
                spot = (part * 2 + cc) * n + d
                total = total + recv2[spot].astype(jnp.int32).astype(F32) * rgrain[spot][:, 0:1]
            t8s[:, span] = total
            moved = total * risks[:, span]
            _, low = split_pair(moved)
            pieces = jnp.concatenate([moved, low], 0).astype(BF16)
            for hi in range(hi_n):
                lhs[hi * 16 : hi * 16 + 16, span] = pieces * hrep[hi, :, span]
    inside = lax.dot_general(
        lhs[...], m1[...], over_both, preferred_element_type=F32
    ).reshape(hi_n, 16, LO)
    inside_t = inside[:, 0:8] + inside[:, 8:16]
    carry_t = [None] * hi_n
    sum_t = jnp.zeros((8, 1), F32)
    for hi in range(hi_n - 1, -1, -1):
        carry_t[hi] = sum_t
        sum_t = sum_t + inside_t[hi][:, 0:1]

    left(zr1.at[pl.ds(0, nz - 1)], 8)
    landed(zr1.at[pl.ds(0, nz - 1)], 8)
    own_later = jnp.zeros(one, F32)
    for zz in range(nz):
        own_later = own_later + jnp.where(zz > z, zr1[zz], 0.0)

    at_risk = at_local + own_later[:, 0:1]
    hazard = happened / at_risk
    slope = happened / (at_risk * at_risk)
    before_h, _ = scan_hi(jnp.sum(hazard, axis=1, keepdims=True), True)
    before_g, sum_g = scan_hi(jnp.sum(slope, axis=1, keepdims=True), True)

    run_t = jnp.zeros((8, 1), F32)
    before, rates = [], []
    for hi in range(hi_n):
        row_h = jnp.broadcast_to(hazard[hi : hi + 1], (4, LO))
        row_g = jnp.broadcast_to(slope[hi : hi + 1], (8, LO))
        hazard_t = (inside_t[hi] + carry_t[hi]) * row_g
        before.append(
            jnp.concatenate(
                [
                    run_t,
                    jnp.broadcast_to(before_h[hi : hi + 1], (4, 1)),
                    jnp.broadcast_to(before_g[hi : hi + 1], (4, 1)),
                ],
                0,
            )
        )
        rates += [hazard_t, row_h, row_g[0:4]]
        run_t = run_t + jnp.sum(hazard_t, axis=1, keepdims=True)

    def exchange_past():
        left(zw.at[pl.ds(0, nz - 1)], 9)
        landed(zw.at[pl.ds(0, nz - 1)], 9)
        later = jnp.zeros(one, F32)
        past = jnp.zeros(wide, F32)
        for zz in range(nz - 1, -1, -1):
            level = zw[zz].astype(jnp.int32).astype(F32)
            share = 1.0 / (level * (zr1[zz][:, 0:1] * (1.0 / STEPS)) + later[:, 0:1])
            past = past + jnp.where(level >= 0.0, jnp.where(zz < z, share, 0.0), 0.0)
            later = later + zr1[zz]
        count = later[:, 1:2]
        past = jnp.sum(jnp.sum(past, axis=0, keepdims=True), axis=1, keepdims=True)
        zc[...] = jnp.broadcast_to(past, one)
        swap_c = remote(zc, zrc, send.at[13], recv.at[13], partner)
        swap_c.start()
        return swap_c, count

    rate, rate_low = split_pair(jnp.concatenate(rates, 0))
    rate_low = rate_low.astype(BF16)
    width = min(512, half)
    for chunk in range(half // width):
        if chunk == half // width // 4:
            swap_c, count = exchange_past()
        begin = pl.multiple_of(c * half + chunk * width, width)
        member = m1[:, pl.ds(begin, width)]
        spread = jnp.dot(rate, member, preferred_element_type=F32) + jnp.dot(
            rate_low, member, preferred_element_type=F32
        )
        spot = hi8[:, pl.ds(begin, width)]
        spot = jnp.concatenate([spot, spot], 0)
        chosen = jnp.zeros((16, width), F32)
        for hi in range(hi_n):
            chosen = jnp.where(spot == hi, spread[hi * 16 : hi * 16 + 16] + before[hi], chosen)
        sel[:, chunk * width : (chunk + 1) * width] = chosen

    lane8 = lax.broadcasted_iota(jnp.int32, (8, 128), 1)

    swap_c.wait()
    early_h = (zc[...] + zrc[...])[:, 0:1]

    tops = []
    for part in range(2):
        span = slice(part * sub, part * sub + sub)
        begin = pl.multiple_of(c * half + part * sub, sub)
        tangent, risk = t8s[:, pl.ds(begin, sub)], risks[:, pl.ds(begin, sub)]
        hazards = jnp.broadcast_to(sel[8:9, span] + early_h, (8, sub))
        weighted = risk * (tangent * hazards - sel[0:8, span])
        top = jnp.maximum(jnp.max(jnp.abs(weighted), axis=1, keepdims=True), 1e-30)
        abuf[part, x, y] = jnp.floor(weighted * (STEPS / top) + 0.5).astype(jnp.int32).astype(jnp.int16)
        tops.append(top * (1.0 / STEPS))
    columns = [sum_t, run_t] + tops
    tile = jnp.broadcast_to(columns[3], (8, 128))
    for place_k in range(3):
        tile = jnp.where(lane8 == place_k, jnp.broadcast_to(columns[place_k], (8, 128)), tile)
    tot[x, y] = tile

    def cross(part, slot_of, k, turn):
        for d in turn:
            device = at(y, xs[d], c) if part == 0 else at(ys[d], x, c)
            for ref, sem in ((abuf.at[part], k),) + (((tot, 19),) if part == 0 else ()):
                remote(slot_of(ref), slot_of(ref), send.at[sem], recv.at[sem], device).start()

    nearest = turn[::-1]
    for part in range(2):
        for d in turn:
            device = at(ys[d], x, c) if part == 0 else at(y, xs[d], c)
            for ref, sem in ((abuf.at[part], 14 + part),) + (((tot, 16),) if part == 0 else ()):
                slot = ref.at[x, y]
                arrive = recv_at.at[(part if sem < 16 else 2) * n + d]
                remote(slot, slot, send.at[sem], arrive, device).start()
    for part in range(2):
        cross(part, lambda ref: ref.at[x, y], 17 + part, turn)
    got = over_persons(risks[:, mine] * jnp.broadcast_to(sel[12:13, :], (8, half)))
    wide_g = jnp.broadcast_to(sum_g, one)
    zu[0] = jnp.concatenate([got[:, :128], wide_g], 1)
    zu[1] = jnp.concatenate([got[:, 128:], wide_g], 1)
    for d in far:
        for cc in (c, other):
            remote(zu.at[cc], zru.at[c * nz + z], send.at[12], recv.at[12], along(zs[d], cc)).start()
    for d in nearest:
        for part in range(2):
            if part == 0:
                spot = (x, lax.rem(y + n - d, n))
            else:
                spot = (lax.rem(x + n - d, n), y)
            for ref, row in ((abuf.at[part], part),) + (((tot, 2),) if part == 0 else ()):
                slot = ref.at[spot[0], spot[1]]
                remote(slot, slot, send.at[14], recv_at.at[row * n + d], partner).wait_recv()
            cross(part, lambda ref: ref.at[spot[0], spot[1]], 17 + part, turn)
    for part in range(2):
        left(abuf.at[part, 0, pl.ds(0, n - 1)], 14 + part)
    left(tot.at[0, pl.ds(0, n - 1)], 16)
    digits = []
    for part in range(2):
        view = abuf.at[part, pl.ds(0, n - 1)]
        left(view, 17 + part)
        landed(view, 17 + part)
        level = abuf[part].reshape(n * n * 8, sub).astype(jnp.int32)
        digits.append(((level >> 8).astype(F32).astype(BF16), (level & 255).astype(F32).astype(BF16)))
    left(tot.at[pl.ds(0, n - 1)], 19)
    landed(tot.at[pl.ds(0, n - 1)], 19)

    k_n = n * n * 8
    totals = tot[...].reshape(k_n, 128)
    def multiply(columns_d):
        product = jnp.zeros((k_n, 128), F32)
        for part in range(2):
            people = d2[part * sub : part * sub + sub, columns_d]
            upper = jnp.dot(digits[part][0], people, preferred_element_type=F32)
            lower = jnp.dot(digits[part][1], people, preferred_element_type=F32)
            product = product + (upper * 256.0 + lower) * totals[:, 2 + part : 3 + part]
        return product

    pbuf[0] = multiply(pl.ds(pl.multiple_of(other * 128, 128), 128))
    swap = remote(pbuf.at[0], prec, send.at[20], recv.at[20], partner)
    swap.start()
    product = multiply(lanes)
    left(zrq.at[pl.ds(0, 2 * nz - 1)], 11)
    landed(zrq.at[pl.ds(0, 2 * nz - 1)], 11)
    left(zru.at[pl.ds(0, 2 * nz - 2)], 12)
    landed(zru.at[pl.ds(0, 2 * nz - 2)], 12)
    beyond = jnp.zeros(one, F32)
    before_u = jnp.zeros(one, F32)
    after_q = jnp.zeros(one, F32)
    for zz in range(nz - 1, -1, -1):
        risk_sum = zrq[zz] + zrq[nz + zz]
        slope_sum = zru[zz][:, :128] + zru[nz + zz][:, :128] + zru[zz][:, 128:] * beyond
        before_u = before_u + jnp.where(zz < z, slope_sum, 0.0)
        after_q = after_q + jnp.where(zz > z, risk_sum, 0.0)
        beyond = beyond + risk_sum
    fixed = totals[:, 0:1] * before_u + totals[:, 1:2] * after_q
    swap.wait()
    blocks = nz // 2
    share = k_n // blocks
    mine_b = lax.rem(z, blocks)
    total = (product + prec[...] - fixed).reshape(blocks, share, 128)
    top = jnp.max(jnp.max(jnp.abs(total), axis=1, keepdims=True), axis=2, keepdims=True)
    top = jnp.maximum(top, 1e-30)
    ps[...] = jnp.floor(total * (STEPS / top) + 0.5).astype(jnp.int32).astype(jnp.int16)
    pu[...] = jnp.broadcast_to(top * (1.0 / STEPS), (blocks, 1, 128))
    zr3[z] = ps[mine_b]
    zr3u[z] = pu[mine_b]
    for d in far:
        block = lax.rem(zs[d], blocks)
        remote(pu.at[block], zr3u.at[z], send.at[24], recv.at[24], along(zs[d], c)).start()
        remote(ps.at[block], zr3.at[z], send.at[21], recv.at[21], along(zs[d], c)).start()
    left(zr3.at[pl.ds(0, nz - 1)], 21)
    landed(zr3.at[pl.ds(0, nz - 1)], 21)
    left(zr3u.at[pl.ds(0, nz - 1)], 24)
    landed(zr3u.at[pl.ds(0, nz - 1)], 24)
    done = jnp.zeros((share, 128), F32)
    for zz in range(nz):
        done = done + zr3[zz].astype(jnp.int32).astype(F32) * zr3u[zz]
    obuf[mine_b] = done / count
    near = [d for d in far if d <= blocks // 2 or nz - d < blocks // 2]
    for d in near:
        slot = obuf.at[mine_b]
        remote(slot, slot, send.at[22], recv.at[22], along(zs[d], c)).start()
    if len(near) > 0:
        left(obuf.at[pl.ds(0, blocks - 1)], 22)
        landed(obuf.at[pl.ds(0, blocks - 1)], 22)
    out_ref[...] = obuf[...].reshape(k_n, 128).T


def local(nz, n, dosages, coefficients, directions, event_rank, events):
    rows, feats = dosages.shape
    k_n = directions.shape[1]
    sub, half, hi_n = rows // 4, rows // 2, rows // LO
    vmem = pl.BlockSpec(memory_space=pltpu.VMEM)
    dma = pltpu.SemaphoreType.DMA
    return pl.pallas_call(
        functools.partial(kernel, nz, n),
        out_shape=jax.ShapeDtypeStruct((feats, k_n), F32),
        in_specs=[pl.BlockSpec(memory_space=pltpu.HBM)] * 5,
        out_specs=vmem,
        scratch_shapes=[
            pltpu.VMEM((rows // 128, 128), jnp.int32),
            pltpu.VMEM((rows // 128, 128), jnp.int32),
            pltpu.VMEM((rows, feats), BF16),
            pltpu.VMEM((half, 2 * feats), BF16),
            pltpu.VMEM((2, feats, k_n), BF16),
            pltpu.VMEM((1, feats), BF16),
            pltpu.VMEM((2, n, n, 8, sub), F32),
            pltpu.VMEM((2, n, n, 8, sub), jnp.int16),
            pltpu.VMEM((2, 1, 128), F32),
            pltpu.VMEM((2 * n, 1, 128), F32),
            pltpu.VMEM((1, rows), F32),
            pltpu.VMEM((1, half), F32),
            pltpu.VMEM((1, half), F32),
            pltpu.VMEM((2, n, n, 8, sub), jnp.int16),
            pltpu.VMEM((n, 1, half), F32),
            pltpu.VMEM((2, n, 8, sub), jnp.int16),
            pltpu.VMEM((2, 1, 128), F32),
            pltpu.VMEM((4 * n, 1, 128), F32),
            pltpu.VMEM((1, half), F32),
            pltpu.VMEM((4 * n, 8, sub), jnp.int16),
            pltpu.VMEM((2 * n, 1, half), F32),
            pltpu.VMEM((LO, rows), BF16),
            pltpu.VMEM((hi_n, 16, rows), BF16),
            pltpu.VMEM((8, rows), jnp.int32),
            pltpu.VMEM((hi_n * 16, rows), BF16),
            pltpu.VMEM((hi_n * 2, rows), BF16),
            pltpu.VMEM((8, rows), F32),
            pltpu.VMEM((8, rows), F32),
            pltpu.VMEM((16, half), F32),
            pltpu.VMEM((nz, 1, 128), F32),
            pltpu.VMEM((nz, hi_n, 128), jnp.int16),
            pltpu.VMEM((1, 128), F32),
            pltpu.VMEM((1, 128), F32),
            pltpu.VMEM((2, 1, 128), F32),
            pltpu.VMEM((2 * nz, 1, 128), F32),
            pltpu.VMEM((2, 1, 256), F32),
            pltpu.VMEM((2 * nz, 1, 256), F32),
            pltpu.VMEM((n, n, 8, 128), F32),
            pltpu.VMEM((2, n, n, 8, sub), jnp.int16),
            pltpu.VMEM((1, k_n, 128), F32),
            pltpu.VMEM((k_n, 128), F32),
            pltpu.VMEM((nz // 2, k_n * 2 // nz, 128), jnp.int16),
            pltpu.VMEM((nz // 2, 1, 128), F32),
            pltpu.VMEM((nz, k_n * 2 // nz, 128), jnp.int16),
            pltpu.VMEM((nz, 1, 128), F32),
            pltpu.VMEM((nz // 2, k_n * 2 // nz, 128), F32),
            dma((6,)),
            dma((25,)),
            dma((25,)),
            dma((3 * n,)),
        ],
        compiler_params=pltpu.CompilerParams(
            collective_id=0, has_side_effects=True, vmem_limit_bytes=VMEM_MIB * 2**20
        ),
        name="cox",
    )(
        *(
            pltpu.with_memory_space_constraint(a, pltpu.HBM)
            for a in (
                dosages,
                coefficients.reshape(1, feats),
                directions,
                event_rank.reshape(rows // 128, 128),
                events.reshape(rows // 128, 128),
            )
        )
    )


def solution(mesh):
    nz, chips = mesh.shape["ex"], mesh.shape["feat"] // 2
    n = round(chips**0.5)
    placed = (P("ex", "feat"), P("feat"), P("feat", None), P("ex"), P("ex"))
    return jax.shard_map(
        functools.partial(local, nz, n), mesh=mesh, in_specs=placed, out_specs=P("feat", None), check_vma=False
    )
```
